256 devices in a mesh: frames: 8 (over x, core), rows: 32 (over y, z).
Axes of the slice: x: 4, y: 4, z: 8, core: 2. Of those that a mesh axis runs over, the one named last changes fastest.
Arguments:
- observed: float32 [32, 2048, 2048], P('frames', 'rows'), may hold values from 0.25 to 4
- kernel: float32 [2048, 65], P('rows'), may hold values from 0.004 to 0.04
- row_shift: int32 [2048], P('rows'), may hold values from -8 to 8
- cycle_map: float32 [2048, 256], P('rows'), may hold values from 0 to 0.03125
- cycle_blocks: int32 [32, 8], P('rows'), may hold values from 0 to 63
- chi_map: bfloat16 [32, 2048, 720], P('rows'), may hold values from 0 to 3.0517578e-05
Outputs:
- binned: float32 [2048, 720], P('rows')
The draws below stay inside these ranges and needn't reach their ends.
All inputs are finite; a program needn't handle non-finite values.
Results may differ from the reference program's by a relative error of at most 0.0003.
Values sent between devices are 32-bit elements; how exact they have to be, the bound alone decides.
A program may use at most 128 MiB of HBM per device.

```python
import math
import jax
import jax.numpy as jnp
from jax import lax

COLS = 2048
ROWS_DEV = 64
F_DEV = 4
BAND = 65
SHIFT = 8
ITERS = 4
Q = 2048
CHI = 720
QB = 32
NB = 8
HALO = 40
TILES = 32
ROWS = 2048
FRAMES = 32
BLOCKS = 64
N_FRAMES = 8


def draw_row_shift(key, part):
    values = jax.random.randint(key, (ROWS,), -SHIFT, SHIFT + 1, dtype=jnp.int32)
    values = values.at[0].set(SHIFT)
    values = values.at[1].set(-SHIFT)
    return values


def draw_cycle_blocks(key, part):
    values = jax.random.randint(key, (TILES, NB), 0, BLOCKS, dtype=jnp.int32)
    values = values.at[0, 0].set(0)
    values = values.at[0, 1].set(BLOCKS - 1)
    return values


def block_scale(rng, shape, split, smallest, high):
    factor_of = 1.0
    for position, blocks in split:
        draws = jax.random.uniform(jax.random.fold_in(jax.random.fold_in(rng, 6), position), (blocks,), jnp.float32, smallest / len(split), high / len(split))
        factor_of = factor_of * jnp.repeat(jnp.exp(draws), shape[position] // blocks).reshape((-1,) + (1,) * (len(shape) - 1 - position))
    return factor_of


def setup_inputs(seed: int = 0) -> dict:
    keys = jax.random.split(jax.random.key(seed), 7)
    observed = jnp.clip(jnp.exp(math.log(4.0) - 2.7725887 * jax.random.uniform(keys[0], (FRAMES, ROWS, COLS), jnp.float32) ** block_scale(keys[0], (FRAMES, ROWS, COLS), ((0, 8), (1, 32)), -0.2, 0.2)), 0.25, 4.0)
    kernel = jnp.clip(jnp.exp(math.log(0.04) - 2.30258502 * jax.random.uniform(keys[1], (ROWS, BAND), jnp.float32) ** block_scale(keys[1], (ROWS, BAND), ((0, 32),), -0.2, 0.2)), 0.004, 0.04)
    row_shift = draw_row_shift(jax.random.fold_in(keys[6], 71), 0)
    cycle_map = jnp.clip(0.03125 * jax.random.uniform(keys[3], (ROWS, NB * QB), jnp.float32) ** block_scale(keys[3], (ROWS, NB * QB), ((0, 32),), -0.2, 0.2), 0.0, 0.03125)
    cycle_blocks = draw_cycle_blocks(jax.random.fold_in(keys[6], 71), 0)
    chi_map = jnp.clip(3.0517578125e-05 * jax.random.uniform(keys[5], (TILES, COLS, CHI), jnp.float32) ** block_scale(keys[5], (TILES, COLS, CHI), ((0, 32),), -0.2, 0.2), 0.0, 3.0517578125e-05).astype(jnp.bfloat16)
    return {"observed": observed, "kernel": kernel, "row_shift": row_shift, "cycle_map": cycle_map, "cycle_blocks": cycle_blocks, "chi_map": chi_map}


def band_matrix(kernel, row_shift, first_row, total_rows, halo_rows):
    rows_here = kernel.shape[0]
    band_width = kernel.shape[1]
    half_band = (band_width - 1) // 2
    local_rows = jnp.arange(rows_here, dtype=jnp.int32)[:, None]
    tap_index = jnp.arange(band_width, dtype=jnp.int32)[None, :]
    target = local_rows + row_shift[:, None] + tap_index - half_band
    global_rows = target + first_row
    inside = (global_rows >= 0) & (global_rows < total_rows)
    weights = jnp.where(inside, kernel, jnp.float32(0.0))
    columns = jnp.arange(rows_here + 2 * halo_rows, dtype=jnp.int32)
    matches = (target[:, :, None] + halo_rows == columns[None, None, :]).astype(jnp.float32)
    return jnp.einsum("ik,ikj->ij", weights, matches, precision=lax.Precision.HIGHEST)


def reference(observed, kernel, row_shift, cycle_map, cycle_blocks, chi_map):
    tile_ids = jnp.arange(TILES, dtype=jnp.int32)

    def make_band(tile):
        first_row = (tile * ROWS_DEV).astype(jnp.int32)
        kernel_rows = lax.dynamic_slice_in_dim(kernel, first_row, ROWS_DEV, 0)
        shift_rows = lax.dynamic_slice_in_dim(row_shift, first_row, ROWS_DEV, 0)
        return band_matrix(kernel_rows, shift_rows, first_row, ROWS, HALO)

    band_all = lax.map(make_band, tile_ids)

    def forward(field):
        padded = jnp.pad(field, ((HALO, HALO), (0, 0)))

        def one_tile(tile):
            window = lax.dynamic_slice_in_dim(padded, (tile * ROWS_DEV).astype(jnp.int32), ROWS_DEV + 2 * HALO, 0)
            return jnp.dot(band_all[tile], window, precision=lax.Precision.HIGHEST)

        return lax.map(one_tile, tile_ids).reshape(ROWS, field.shape[1])

    def adjoint(values):
        def one_tile(tile):
            piece = lax.dynamic_slice_in_dim(values, (tile * ROWS_DEV).astype(jnp.int32), ROWS_DEV, 0)
            return jnp.dot(band_all[tile].T, piece, precision=lax.Precision.HIGHEST)

        contrib = lax.map(one_tile, tile_ids)

        def add_tile(tile, total):
            start = (tile * ROWS_DEV).astype(jnp.int32)
            piece = lax.dynamic_slice_in_dim(total, start, ROWS_DEV + 2 * HALO, 0)
            return lax.dynamic_update_slice_in_dim(total, piece + contrib[tile], start, 0)

        total = lax.fori_loop(0, TILES, add_tile, jnp.zeros((ROWS + 2 * HALO, values.shape[1]), jnp.float32))
        return total[HALO:HALO + ROWS]

    norm_sums = adjoint(jnp.ones((ROWS, 1), jnp.float32))

    def restore(frame):
        estimate = frame
        for repeat in range(ITERS):
            estimate = estimate * adjoint(frame / forward(estimate)) / norm_sums
        return estimate

    restored = lax.map(restore, observed)
    group_sums = jnp.sum(restored.reshape(N_FRAMES, F_DEV, ROWS, COLS), axis=1)

    def bin_tile(total, tile):
        start = (tile * ROWS_DEV).astype(jnp.int32)
        tile_sums = lax.dynamic_slice_in_dim(group_sums, start, ROWS_DEV, 1)
        cycle_rows = lax.dynamic_slice_in_dim(cycle_map, start, ROWS_DEV, 0)
        parts = jnp.einsum("rq,grc->gqc", cycle_rows, tile_sums, precision=lax.Precision.HIGHEST).astype(jnp.bfloat16)
        merged = jnp.sum(parts.astype(jnp.float32), axis=0)
        blocks = jnp.dot(merged, chi_map[tile].astype(jnp.float32), precision=lax.Precision.HIGHEST).reshape(NB, QB, CHI)
        onehot = (jnp.arange(BLOCKS, dtype=jnp.int32)[:, None] == cycle_blocks[tile][None, :]).astype(jnp.float32)
        placed = jnp.einsum("kb,bqc->kqc", onehot, blocks, precision=lax.Precision.HIGHEST).reshape(Q, CHI)
        return total + placed, None

    binned = lax.scan(bin_tile, jnp.zeros((Q, CHI), jnp.float32), tile_ids)[0]
    return binned
```

```python
import functools

import jax
import jax.numpy as jnp
from jax import lax
from jax.experimental import pallas as pl
from jax.experimental.pallas import tpu as pltpu
from jax.sharding import PartitionSpec as P

NY, NZ, NX, NC = 4, 8, 4, 2
TILES, GROUPS = NY * NZ, NX * NC
ROWS, COLS, TILE = 2048, 2048, 64
F_DEV, BAND, SHIFT, ITERS = 4, 65, 8, 4
REACH = (BAND - 1) // 2 + SHIFT
CHI, QB, NB = 720, 32, 8
BLK = 128
FRONT = 48
PADDED = ROWS + 2 * BLK - BLK
KBLKS = ROWS // BLK
CHIP = 768

F32, BF16 = jnp.float32, jnp.bfloat16
MESH = pl.DeviceIdType.MESH
VMEM_LIMIT = 60 * 1024 * 1024

OTHERS = [(dy, dz) for dz in (4, -3, 3, -2, 2, -1, 1, 0) for dy in (2, 1, -1, 0) if (dy, dz) != (0, 0)]


def position():
    group = lax.axis_index("frames")
    tile = lax.axis_index("rows")
    return group, tile, tile // NZ, lax.rem(tile, NZ)


def other_tile(y, z, offset):
    return lax.rem(y + offset[0] + NY, NY) * NZ + lax.rem(z + offset[1] + NZ, NZ)


def greet(group, y, z):
    barrier = pltpu.get_barrier_semaphore()
    for offset in OTHERS:
        pl.semaphore_signal(barrier, inc=1, device_id={"rows": other_tile(y, z, offset)}, device_id_type=MESH)
    for step in range(1, GROUPS):
        pl.semaphore_signal(barrier, inc=1, device_id={"frames": lax.rem(group + step, GROUPS)}, device_id_type=MESH)
    return barrier, len(OTHERS) + GROUPS - 1


def lanes(shape):
    return lax.broadcasted_iota(jnp.int32, shape, len(shape) - 1)


def sublanes(shape):
    return lax.broadcasted_iota(jnp.int32, shape, len(shape) - 2)


def halves(value):
    high = value.astype(BF16)
    return high, (value - high.astype(F32)).astype(BF16)


def remote(src, dst, send_sem, recv_sem, device):
    return pltpu.make_async_remote_copy(
        src_ref=src, dst_ref=dst, send_sem=send_sem, recv_sem=recv_sem, device_id=device, device_id_type=MESH
    )


def transpose_kernel(obs, kern, shift, columns, bands, packed, taps, send_a, recv_a, send_b, recv_b, send_c, recv_c):
    group, tile, y, z = position()
    barrier, greeted = greet(group, y, z)
    per = TILE // GROUPS

    taps[...] = jnp.zeros_like(taps)
    taps[:, :BAND] = kern[pl.ds(pl.multiple_of(group * per, per), per), :]
    rows_of = sublanes((per, BLK))
    moves = jnp.zeros((per, BLK), jnp.int32)
    for r in range(per):
        moves = jnp.where(rows_of == r, shift[group * per + r] + SHIFT, moves)
    plain = taps[...]
    moved = jnp.zeros((per, BLK), F32)
    for s in range(2 * SHIFT + 1):
        moved = jnp.where(moves == s, pltpu.roll(plain, s, 1) if s else plain, moved)
    target = tile * TILE + group * per + rows_of + lanes((per, BLK)) - REACH
    moved = jnp.where((target >= 0) & (target < ROWS), moved, 0.0)
    bands[tile, group] = moved

    left = lanes((TILE, BLK)) < BLK // 2

    @pl.loop(0, COLS // BLK)
    def _(m):
        part = [obs[f, :, pl.ds(pl.multiple_of(m * BLK, BLK), BLK)] for f in range(F_DEV)]
        turned = [pltpu.roll(p, BLK // 2, 1) for p in part]
        for pair in range(2):
            a, b = 2 * pair, 2 * pair + 1
            packed[2 * m, :, pair * BLK : (pair + 1) * BLK] = jnp.where(left, part[a], turned[b])
            packed[2 * m + 1, :, pair * BLK : (pair + 1) * BLK] = jnp.where(left, turned[a], part[b])

    columns[tile] = packed[tile]
    pl.semaphore_wait(barrier, greeted)

    first, big, last = [], [], []
    for n, offset in enumerate(OTHERS):
        copy = remote(bands.at[tile, group], bands.at[tile, group], send_b.at[n], recv_b.at[n], {"rows": other_tile(y, z, offset)})
        copy.start()
        first.append(copy)
    for n, offset in enumerate(OTHERS):
        to = other_tile(y, z, offset)
        copy = remote(packed.at[to], columns.at[tile], send_a.at[n], recv_a.at[n], {"rows": to})
        copy.start()
        big.append(copy)
    for copy in first:
        copy.wait()
    for step in range(1, GROUPS):
        to = lax.rem(group + step, GROUPS)
        copy = remote(bands.at[:, group], bands.at[:, group], send_c.at[step - 1], recv_c.at[step - 1], {"frames": to})
        copy.start()
        last.append(copy)
    for copy in big + last:
        copy.wait()


def restore_kernel(obs, taps, out, wide, fwd, adj, est, est_hi, est_lo, rat_hi, rat_lo):
    wide[0:FRONT, :] = jnp.zeros((FRONT, BLK), F32)
    wide[FRONT + ROWS :, :] = jnp.zeros((PADDED - FRONT - ROWS, BLK), F32)
    wide[FRONT : FRONT + ROWS, :] = taps[...]
    for ref in (est_hi, est_lo, rat_hi, rat_lo):
        ref[0:FRONT, :] = jnp.zeros((FRONT, 2 * BLK), BF16)
        ref[FRONT + ROWS :, :] = jnp.zeros((PADDED - FRONT - ROWS, 2 * BLK), BF16)

    @pl.loop(0, KBLKS)
    def _(k):
        row = pl.multiple_of(k * BLK, BLK)
        mine = wide[pl.ds(row + FRONT, BLK), :]
        mine = jnp.concatenate([mine, jnp.zeros_like(mine)], axis=1)
        mine = pltpu.roll(mine, FRONT - REACH, 1, stride=1, stride_axis=0)
        high, low = halves(mine)
        fwd[k, 0:BLK, :] = high
        fwd[k, BLK:, :] = low
        near = wide[pl.ds(row, 2 * BLK), :]
        near = jnp.concatenate([near, jnp.zeros_like(near)], axis=1)
        near = pltpu.roll(near, 2 * BLK - (FRONT + REACH), 1, stride=1, stride_axis=0)[:, :BLK]
        near = near / jnp.sum(near, axis=0, keepdims=True)
        high, low = halves(jnp.transpose(near))
        adj[k, 0:BLK, :] = high
        adj[k, BLK:, :] = low
        start = obs[pl.ds(row, BLK), :]
        est[pl.ds(row, BLK), :] = start
        high, low = halves(start)
        est_hi[pl.ds(row + FRONT, BLK), :] = high
        est_lo[pl.ds(row + FRONT, BLK), :] = low

    def product(mat, k, row, hi, lo):
        both = jnp.dot(mat[k], hi[pl.ds(row, 2 * BLK), :], preferred_element_type=F32)
        rest = jnp.dot(mat[k, 0:BLK, :], lo[pl.ds(row, 2 * BLK), :], preferred_element_type=F32)
        return both[:BLK] + (both[BLK:] + rest)

    def forward():
        @pl.loop(0, KBLKS)
        def _(k):
            row = pl.multiple_of(k * BLK, BLK)
            ratio = obs[pl.ds(row, BLK), :] / product(fwd, k, row, est_hi, est_lo)
            high, low = halves(ratio)
            rat_hi[pl.ds(row + FRONT, BLK), :] = high
            rat_lo[pl.ds(row + FRONT, BLK), :] = low

    @pl.loop(0, ITERS - 1)
    def _(repeat):
        forward()

        @pl.loop(0, KBLKS)
        def _(k):
            row = pl.multiple_of(k * BLK, BLK)
            value = est[pl.ds(row, BLK), :] * product(adj, k, row, rat_hi, rat_lo)
            est[pl.ds(row, BLK), :] = value
            high, low = halves(value)
            est_hi[pl.ds(row + FRONT, BLK), :] = high
            est_lo[pl.ds(row + FRONT, BLK), :] = low

    forward()
    left = lanes((TILE // 2, BLK)) < BLK // 2

    @pl.loop(0, KBLKS)
    def _(k):
        row = pl.multiple_of(k * BLK, BLK)
        value = est[pl.ds(row, BLK), :] * product(adj, k, row, rat_hi, rat_lo)
        value = value[:, :BLK] + value[:, BLK:]
        value = value + pltpu.roll(value, BLK // 2, 1)
        for half in range(2):
            top = half * TILE
            out[2 * k + half] = jnp.where(left, value[top : top + TILE // 2], value[top + TILE // 2 : top + TILE])


def bin_kernel(
    parts, cyc, ids, chi_hbm, out, chi, got, summed, shared, from_core, mixed, from_x, named, around, placed, from_z, own, final,
    chi_sem, send_a, recv_a, send_c, recv_c, send_x, recv_x, send_y, recv_y, send_z, recv_z, send_g, recv_g,
):
    group, tile, y, z = position()
    x, core = group // NC, lax.rem(group, NC)
    load = pltpu.make_async_copy(chi_hbm.at[0], chi, chi_sem)
    load.start()
    barrier, greeted = greet(group, y, z)

    share = QB // GROUPS
    q = sublanes((NB * QB, NB * QB))
    wanted = ((q // share) % NB) * QB + (q // QB) * share + q % share
    order = (lanes((NB * QB, NB * QB)) == wanted).astype(BF16)
    turn = functools.partial(lax.dot_general, dimension_numbers=(((1,), (1,)), ((), ())), preferred_element_type=F32)
    high, low = halves(cyc[...])
    high, low = turn(order, high).astype(BF16), turn(order, low).astype(BF16)
    weights = jnp.concatenate([high, high, low], axis=1)
    got[tile] = parts[tile]
    pl.semaphore_wait(barrier, greeted)

    copies = []
    for n, offset in enumerate(OTHERS):
        to = other_tile(y, z, offset)
        copy = remote(parts.at[to], got.at[tile], send_a.at[n], recv_a.at[n], {"rows": to})
        copy.start()
        copies.append(copy)
    for copy in copies:
        copy.wait()

    left = lanes((TILE // 2, BLK)) < BLK // 2
    for m in range(COLS // BLK):
        a, b = got[2 * m], got[2 * m + 1]
        summed[0 : TILE // 2, m * BLK : (m + 1) * BLK] = jnp.where(left, a, pltpu.roll(b, BLK // 2, 1))
        summed[TILE // 2 :, m * BLK : (m + 1) * BLK] = jnp.where(left, pltpu.roll(a, BLK // 2, 1), b)
    load.wait()
    total = jnp.zeros((NB * QB, CHI), F32)
    step = COLS // 4
    for m in range(4):
        high, low = halves(summed[:, m * step : (m + 1) * step])
        part = jnp.dot(weights, jnp.concatenate([high, low, high], axis=0), preferred_element_type=F32).astype(BF16)
        total = total + jnp.dot(part, chi[m * step : (m + 1) * step, :], preferred_element_type=F32)
    for i in range(NX):
        for j in range(NC):
            top = (i * NC + j) * QB
            shared[j, i] = total[top : top + QB]

    swap = remote(shared.at[1 - core], from_core, send_c, recv_c, {"frames": x * NC + 1 - core})
    swap.start()
    swap.wait()
    mixed[...] = shared[core] + from_core[...]
    copies = []
    for n in range(1, NX):
        to = lax.rem(x + n, NX)
        copy = remote(mixed.at[to], from_x.at[n - 1], send_x.at[n - 1], recv_x.at[n - 1], {"frames": to * NC + core})
        copy.start()
        copies.append(copy)
    for copy in copies:
        copy.wait()
    value = mixed[x] + from_x[0] + from_x[1] + from_x[2]

    last = CHIP - BLK
    named[:, 0:last] = value[:, 0:last]
    lane, sub = lanes((QB, BLK)), sublanes((QB, BLK))
    label = jnp.zeros((QB, BLK), jnp.int32)
    for b in range(NB):
        label = jnp.where(sub // share == b, ids[0, b], label)
    tail = jnp.concatenate([value[:, last:], jnp.zeros((QB, CHIP - CHI), F32)], axis=1)
    named[:, last:] = jnp.where(lane == CHI - last, label.astype(F32), tail)
    around[y] = named[...]
    copies = []
    for n in range(1, NY):
        to = lax.rem(y + n, NY) * NZ + z
        copy = remote(named, around.at[y], send_y.at[n - 1], recv_y.at[n - 1], {"rows": to})
        copy.start()
        copies.append(copy)
    for copy in copies:
        copy.wait()

    every = around[...].reshape(NY * QB, CHIP)
    label = every[:, CHI : CHI + 1]
    rows_of, slot = sublanes((NY * QB, NZ * 2 * share)), lanes((NY * QB, NZ * 2 * share))
    owner_block = 2 * (y * NZ) + slot // share
    hit = (label == owner_block.astype(F32)) & (rows_of % share == slot % share)
    hit = hit.astype(BF16)
    high, low = halves(every)
    low2 = (every - high.astype(F32) - low.astype(F32)).astype(BF16)
    place = functools.partial(lax.dot_general, dimension_numbers=(((0,), (0,)), ((), ())), preferred_element_type=F32)
    put = place(jnp.concatenate([hit, hit, hit], axis=0), jnp.concatenate([high, low, low2], axis=0))
    for k in range(NZ):
        placed[k] = put[k * 2 * share : (k + 1) * 2 * share, :CHI]
    copies = []
    for n in range(1, NZ):
        to = lax.rem(z + n, NZ)
        copy = remote(placed.at[to], from_z.at[n - 1], send_z.at[n - 1], recv_z.at[n - 1], {"rows": y * NZ + to})
        copy.start()
        copies.append(copy)
    for copy in copies:
        copy.wait()
    value = placed[z]
    for n in range(NZ - 1):
        value = value + from_z[n]
    own[...] = value
    final[group] = value
    copies = []
    for n in range(1, GROUPS):
        copy = remote(own, final.at[group], send_g.at[n - 1], recv_g.at[n - 1], {"frames": lax.rem(group + n, GROUPS)})
        copy.start()
        copies.append(copy)
    for copy in copies:
        copy.wait()
    low_half = sublanes((2 * share, CHI)) < share
    for j in range(GROUPS // 2):
        a, b = final[2 * j], final[2 * j + 1]
        out[8 * j : 8 * j + 8, :] = jnp.where(low_half, a, pltpu.roll(b, share, 0))
        out[QB + 8 * j : QB + 8 * j + 8, :] = jnp.where(low_half, pltpu.roll(a, share, 0), b)


def body(observed, kernel, row_shift, cycle_map, cycle_blocks, chi_map):
    vmem = pl.BlockSpec(memory_space=pltpu.VMEM)
    smem = pl.BlockSpec(memory_space=pltpu.SMEM)
    dma = pltpu.SemaphoreType.DMA
    count = len(OTHERS)
    columns, bands = pl.pallas_call(
        transpose_kernel,
        name="transpose",
        out_shape=(
            jax.ShapeDtypeStruct((TILES, TILE, 2 * BLK), F32),
            jax.ShapeDtypeStruct((TILES, GROUPS, TILE // GROUPS, BLK), F32),
        ),
        in_specs=[vmem, vmem, smem],
        out_specs=(vmem, vmem),
        scratch_shapes=[
            pltpu.VMEM((TILES, TILE, 2 * BLK), F32),
            pltpu.VMEM((TILE // GROUPS, BLK), F32),
            dma((count,)), dma((count,)), dma((count,)), dma((count,)), dma((GROUPS - 1,)), dma((GROUPS - 1,)),
        ],
        compiler_params=pltpu.CompilerParams(collective_id=0, has_side_effects=True, vmem_limit_bytes=VMEM_LIMIT),
    )(observed, kernel, row_shift)

    parts = pl.pallas_call(
        restore_kernel,
        name="restore",
        out_shape=jax.ShapeDtypeStruct((TILES, TILE // 2, BLK), F32),
        in_specs=[vmem, vmem],
        out_specs=vmem,
        scratch_shapes=[
            pltpu.VMEM((PADDED, BLK), F32),
            pltpu.VMEM((KBLKS, 2 * BLK, 2 * BLK), BF16),
            pltpu.VMEM((KBLKS, 2 * BLK, 2 * BLK), BF16),
            pltpu.VMEM((ROWS, 2 * BLK), F32),
        ]
        + [pltpu.VMEM((PADDED, 2 * BLK), BF16)] * 4,
        compiler_params=pltpu.CompilerParams(vmem_limit_bytes=VMEM_LIMIT),
    )(columns.reshape(ROWS, 2 * BLK), bands.reshape(ROWS, BLK))

    return pl.pallas_call(
        bin_kernel,
        name="bin",
        out_shape=jax.ShapeDtypeStruct((TILE, CHI), F32),
        in_specs=[vmem, vmem, smem, pl.BlockSpec(memory_space=pl.ANY)],
        out_specs=vmem,
        scratch_shapes=[
            pltpu.VMEM((COLS, CHI), BF16),
            pltpu.VMEM((TILES, TILE // 2, BLK), F32),
            pltpu.VMEM((TILE, COLS), F32),
            pltpu.VMEM((NC, NX, QB, CHI), F32),
            pltpu.VMEM((NX, QB, CHI), F32),
            pltpu.VMEM((NX, QB, CHI), F32),
            pltpu.VMEM((NX - 1, QB, CHI), F32),
            pltpu.VMEM((QB, CHIP), F32),
            pltpu.VMEM((NY, QB, CHIP), F32),
            pltpu.VMEM((NZ, 8, CHI), F32),
            pltpu.VMEM((NZ - 1, 8, CHI), F32),
            pltpu.VMEM((8, CHI), F32),
            pltpu.VMEM((GROUPS, 8, CHI), F32),
            dma, dma((count,)), dma((count,)), dma, dma,
            dma((NX - 1,)), dma((NX - 1,)), dma((NY - 1,)), dma((NY - 1,)),
            dma((NZ - 1,)), dma((NZ - 1,)), dma((GROUPS - 1,)), dma((GROUPS - 1,)),
        ],
        compiler_params=pltpu.CompilerParams(collective_id=1, has_side_effects=True, vmem_limit_bytes=VMEM_LIMIT),
    )(parts, cycle_map, cycle_blocks, chi_map)


def solution(mesh):
    return jax.shard_map(
        body,
        mesh=mesh,
        in_specs=(
            P("frames", "rows", None),
            P("rows", None),
            P("rows"),
            P("rows", None),
            P("rows", None),
            P("rows", None, None),
        ),
        out_specs=P("rows", None),
        check_vma=False,
    )
```

```python
import functools

import jax
import jax.numpy as jnp
from jax import lax
from jax.experimental import pallas as pl
from jax.experimental.pallas import tpu as pltpu
from jax.sharding import PartitionSpec as P

NY, NZ, NX, NC = 4, 8, 4, 2
TILES, GROUPS = NY * NZ, NX * NC
ROWS, COLS, TILE = 2048, 2048, 64
F_DEV, BAND, SHIFT, ITERS = 4, 65, 8, 4
REACH = (BAND - 1) // 2 + SHIFT
CHI, QB, NB = 720, 32, 8
BLK = 128
FRONT = 48
PADDED = ROWS + 2 * BLK - BLK
KBLKS = ROWS // BLK
GROUP = 4
CHIP = 768

F32, BF16 = jnp.float32, jnp.bfloat16
MESH = pl.DeviceIdType.MESH
VMEM_LIMIT = 60 * 1024 * 1024

OTHERS = [(dy, dz) for dz in (4, -3, 3, -2, 2, -1, 1, 0) for dy in (2, 1, -1, 0) if (dy, dz) != (0, 0)]


def position():
    group = lax.axis_index("frames")
    tile = lax.axis_index("rows")
    return group, tile, tile // NZ, lax.rem(tile, NZ)


def other_tile(y, z, offset):
    return lax.rem(y + offset[0] + NY, NY) * NZ + lax.rem(z + offset[1] + NZ, NZ)


def greet(group, y, z):
    barrier = pltpu.get_barrier_semaphore()
    for offset in OTHERS:
        pl.semaphore_signal(barrier, inc=1, device_id={"rows": other_tile(y, z, offset)}, device_id_type=MESH)
    for step in range(1, GROUPS):
        pl.semaphore_signal(barrier, inc=1, device_id={"frames": lax.rem(group + step, GROUPS)}, device_id_type=MESH)
    return barrier, len(OTHERS) + GROUPS - 1


def lanes(shape):
    return lax.broadcasted_iota(jnp.int32, shape, len(shape) - 1)


def sublanes(shape):
    return lax.broadcasted_iota(jnp.int32, shape, len(shape) - 2)


def halves(value):
    high = value.astype(BF16)
    return high, (value - high.astype(F32)).astype(BF16)


def remote(src, dst, send_sem, recv_sem, device):
    return pltpu.make_async_remote_copy(
        src_ref=src, dst_ref=dst, send_sem=send_sem, recv_sem=recv_sem, device_id=device, device_id_type=MESH
    )


def transpose_kernel(obs, kern, shift, columns, bands, packed, taps, send_a, recv_a, send_b, recv_b, send_c, recv_c):
    group, tile, y, z = position()
    barrier, greeted = greet(group, y, z)
    per = TILE // GROUPS

    taps[...] = jnp.zeros_like(taps)
    taps[:, :BAND] = kern[pl.ds(pl.multiple_of(group * per, per), per), :]
    rows_of = sublanes((per, BLK))
    moves = jnp.zeros((per, BLK), jnp.int32)
    for r in range(per):
        moves = jnp.where(rows_of == r, shift[group * per + r] + SHIFT, moves)
    plain = taps[...]
    moved = jnp.zeros((per, BLK), F32)
    for s in range(2 * SHIFT + 1):
        moved = jnp.where(moves == s, pltpu.roll(plain, s, 1) if s else plain, moved)
    target = tile * TILE + group * per + rows_of + lanes((per, BLK)) - REACH
    moved = jnp.where((target >= 0) & (target < ROWS), moved, 0.0)
    bands[tile, group] = moved

    left = lanes((TILE, BLK)) < BLK // 2

    @pl.loop(0, COLS // BLK)
    def _(m):
        part = [obs[f, :, pl.ds(pl.multiple_of(m * BLK, BLK), BLK)] for f in range(F_DEV)]
        turned = [pltpu.roll(p, BLK // 2, 1) for p in part]
        for pair in range(2):
            a, b = 2 * pair, 2 * pair + 1
            packed[2 * m, :, pair * BLK : (pair + 1) * BLK] = jnp.where(left, part[a], turned[b])
            packed[2 * m + 1, :, pair * BLK : (pair + 1) * BLK] = jnp.where(left, turned[a], part[b])

    columns[tile] = packed[tile]
    pl.semaphore_wait(barrier, greeted)

    first, big, last = [], [], []
    for n, offset in enumerate(OTHERS):
        copy = remote(bands.at[tile, group], bands.at[tile, group], send_b.at[n], recv_b.at[n], {"rows": other_tile(y, z, offset)})
        copy.start()
        first.append(copy)
    for n, offset in enumerate(OTHERS):
        to = other_tile(y, z, offset)
        copy = remote(packed.at[to], columns.at[tile], send_a.at[n], recv_a.at[n], {"rows": to})
        copy.start()
        big.append(copy)
    for copy in first:
        copy.wait()
    for step in range(1, GROUPS):
        to = lax.rem(group + step, GROUPS)
        copy = remote(bands.at[:, group], bands.at[:, group], send_c.at[step - 1], recv_c.at[step - 1], {"frames": to})
        copy.start()
        last.append(copy)
    for copy in big + last:
        copy.wait()


def restore_kernel(obs, taps, out, wide, fwd, adj, est, est_hi, est_lo, rat_hi, rat_lo):
    wide[0:FRONT, :] = jnp.zeros((FRONT, BLK), F32)
    wide[FRONT + ROWS :, :] = jnp.zeros((PADDED - FRONT - ROWS, BLK), F32)
    wide[FRONT : FRONT + ROWS, :] = taps[...]
    for ref in (est_hi, est_lo, rat_hi, rat_lo):
        ref[0:FRONT, :] = jnp.zeros((FRONT, 2 * BLK), BF16)
        ref[FRONT + ROWS :, :] = jnp.zeros((PADDED - FRONT - ROWS, 2 * BLK), BF16)

    @pl.loop(0, KBLKS)
    def _(k):
        row = pl.multiple_of(k * BLK, BLK)
        mine = wide[pl.ds(row + FRONT, BLK), :]
        mine = jnp.concatenate([mine, jnp.zeros_like(mine)], axis=1)
        mine = pltpu.roll(mine, FRONT - REACH, 1, stride=1, stride_axis=0)
        high, low = halves(mine)
        fwd[k, 0:BLK, :] = high
        fwd[k, BLK:, :] = low
        near = wide[pl.ds(row, 2 * BLK), :]
        near = jnp.concatenate([near, jnp.zeros_like(near)], axis=1)
        near = pltpu.roll(near, 2 * BLK - (FRONT + REACH), 1, stride=1, stride_axis=0)[:, :BLK]
        near = near / jnp.sum(near, axis=0, keepdims=True)
        high, low = halves(jnp.transpose(near))
        adj[k, 0:BLK, :] = high
        adj[k, BLK:, :] = low
        start = obs[pl.ds(row, BLK), :]
        est[pl.ds(row, BLK), :] = start
        high, low = halves(start)
        est_hi[pl.ds(row + FRONT, BLK), :] = high
        est_lo[pl.ds(row + FRONT, BLK), :] = low

    def product(mat, k, row, hi, lo):
        both = jnp.dot(mat[k], hi[pl.ds(row, 2 * BLK), :], preferred_element_type=F32)
        rest = jnp.dot(mat[k, 0:BLK, :], lo[pl.ds(row, 2 * BLK), :], preferred_element_type=F32)
        return both[:BLK] + (both[BLK:] + rest)

    def in_groups(step):
        @pl.loop(0, KBLKS // GROUP)
        def _(g):
            blocks = []
            for j in range(GROUP):
                k = g * GROUP + j
                row = pl.multiple_of(k * BLK, BLK)
                blocks.append((row, step(row, k)))
            for row, store in blocks:
                store(row)

    def store_halves(value, high_ref, low_ref, row):
        high, low = halves(value)
        high_ref[pl.ds(row + FRONT, BLK), :] = high
        low_ref[pl.ds(row + FRONT, BLK), :] = low

    def forward_block(row, k):
        ratio = obs[pl.ds(row, BLK), :] / product(fwd, k, row, est_hi, est_lo)
        return functools.partial(store_halves, ratio, rat_hi, rat_lo)

    def adjoint_block(row, k):
        value = est[pl.ds(row, BLK), :] * product(adj, k, row, rat_hi, rat_lo)

        def store(row):
            est[pl.ds(row, BLK), :] = value
            store_halves(value, est_hi, est_lo, row)

        return store

    @pl.loop(0, ITERS - 1)
    def _(repeat):
        in_groups(forward_block)
        in_groups(adjoint_block)

    in_groups(forward_block)
    left = lanes((TILE // 2, BLK)) < BLK // 2

    def last_block(row, k):
        value = est[pl.ds(row, BLK), :] * product(adj, k, row, rat_hi, rat_lo)
        value = value[:, :BLK] + value[:, BLK:]
        value = value + pltpu.roll(value, BLK // 2, 1)

        def store(row):
            for half in range(2):
                top = half * TILE
                out[2 * k + half] = jnp.where(left, value[top : top + TILE // 2], value[top + TILE // 2 : top + TILE])

        return store

    in_groups(last_block)


def bin_kernel(
    parts, cyc, ids, chi_hbm, out, chi, got, summed, shared, from_core, mixed, from_x, named, around, placed, from_z, own, final,
    chi_sem, send_a, recv_a, send_c, recv_c, send_x, recv_x, send_y, recv_y, send_z, recv_z, send_g, recv_g,
):
    group, tile, y, z = position()
    x, core = group // NC, lax.rem(group, NC)
    load = pltpu.make_async_copy(chi_hbm.at[0], chi, chi_sem)
    load.start()
    barrier, greeted = greet(group, y, z)

    share = QB // GROUPS
    q = sublanes((NB * QB, NB * QB))
    wanted = ((q // share) % NB) * QB + (q // QB) * share + q % share
    order = (lanes((NB * QB, NB * QB)) == wanted).astype(BF16)
    turn = functools.partial(lax.dot_general, dimension_numbers=(((1,), (1,)), ((), ())), preferred_element_type=F32)
    high, low = halves(cyc[...])
    high, low = turn(order, high).astype(BF16), turn(order, low).astype(BF16)
    weights = jnp.concatenate([high, high, low], axis=1)
    got[tile] = parts[tile]
    pl.semaphore_wait(barrier, greeted)

    copies = []
    for n, offset in enumerate(OTHERS):
        to = other_tile(y, z, offset)
        copy = remote(parts.at[to], got.at[tile], send_a.at[n], recv_a.at[n], {"rows": to})
        copy.start()
        copies.append(copy)
    for copy in copies:
        copy.wait()

    left = lanes((TILE // 2, BLK)) < BLK // 2
    for m in range(COLS // BLK):
        a, b = got[2 * m], got[2 * m + 1]
        summed[0 : TILE // 2, m * BLK : (m + 1) * BLK] = jnp.where(left, a, pltpu.roll(b, BLK // 2, 1))
        summed[TILE // 2 :, m * BLK : (m + 1) * BLK] = jnp.where(left, pltpu.roll(a, BLK // 2, 1), b)
    load.wait()
    turn_chi = functools.partial(lax.dot_general, dimension_numbers=(((1,), (1,)), ((), ())), preferred_element_type=F32)
    total = jnp.zeros((NB * QB, CHI), F32)
    step = COLS // 4
    for m in range(4):
        high, low = halves(summed[:, m * step : (m + 1) * step])
        part = jnp.dot(weights, jnp.concatenate([high, low, high], axis=0), preferred_element_type=F32).astype(BF16)
        total = total + turn_chi(part, chi[:, m * step : (m + 1) * step])
    for i in range(NX):
        for j in range(NC):
            top = (i * NC + j) * QB
            shared[j, i] = total[top : top + QB]

    swap = remote(shared.at[1 - core], from_core, send_c, recv_c, {"frames": x * NC + 1 - core})
    swap.start()
    swap.wait()
    mixed[...] = shared[core] + from_core[...]
    copies = []
    for n in range(1, NX):
        to = lax.rem(x + n, NX)
        copy = remote(mixed.at[to], from_x.at[n - 1], send_x.at[n - 1], recv_x.at[n - 1], {"frames": to * NC + core})
        copy.start()
        copies.append(copy)
    for copy in copies:
        copy.wait()
    value = mixed[x] + from_x[0] + from_x[1] + from_x[2]

    last = CHIP - BLK
    named[:, 0:last] = value[:, 0:last]
    lane, sub = lanes((QB, BLK)), sublanes((QB, BLK))
    label = jnp.zeros((QB, BLK), jnp.int32)
    for b in range(NB):
        label = jnp.where(sub // share == b, ids[0, b], label)
    tail = jnp.concatenate([value[:, last:], jnp.zeros((QB, CHIP - CHI), F32)], axis=1)
    named[:, last:] = jnp.where(lane == CHI - last, label.astype(F32), tail)
    around[y] = named[...]
    copies = []
    for n in range(1, NY):
        to = lax.rem(y + n, NY) * NZ + z
        copy = remote(named, around.at[y], send_y.at[n - 1], recv_y.at[n - 1], {"rows": to})
        copy.start()
        copies.append(copy)
    for copy in copies:
        copy.wait()

    every = around[...].reshape(NY * QB, CHIP)
    label = every[:, CHI : CHI + 1]
    rows_of, slot = sublanes((NY * QB, NZ * 2 * share)), lanes((NY * QB, NZ * 2 * share))
    owner_block = 2 * (y * NZ) + slot // share
    hit = (label == owner_block.astype(F32)) & (rows_of % share == slot % share)
    hit = hit.astype(BF16)
    high, low = halves(every)
    low2 = (every - high.astype(F32) - low.astype(F32)).astype(BF16)
    place = functools.partial(lax.dot_general, dimension_numbers=(((0,), (0,)), ((), ())), preferred_element_type=F32)
    put = place(jnp.concatenate([hit, hit, hit], axis=0), jnp.concatenate([high, low, low2], axis=0))
    for k in range(NZ):
        placed[k] = put[k * 2 * share : (k + 1) * 2 * share, :CHI]
    copies = []
    for n in range(1, NZ):
        to = lax.rem(z + n, NZ)
        copy = remote(placed.at[to], from_z.at[n - 1], send_z.at[n - 1], recv_z.at[n - 1], {"rows": y * NZ + to})
        copy.start()
        copies.append(copy)
    for copy in copies:
        copy.wait()
    value = placed[z]
    for n in range(NZ - 1):
        value = value + from_z[n]
    own[...] = value
    final[group] = value
    copies = []
    for n in range(1, GROUPS):
        copy = remote(own, final.at[group], send_g.at[n - 1], recv_g.at[n - 1], {"frames": lax.rem(group + n, GROUPS)})
        copy.start()
        copies.append(copy)
    for copy in copies:
        copy.wait()
    low_half = sublanes((2 * share, CHI)) < share
    for j in range(GROUPS // 2):
        a, b = final[2 * j], final[2 * j + 1]
        out[8 * j : 8 * j + 8, :] = jnp.where(low_half, a, pltpu.roll(b, share, 0))
        out[QB + 8 * j : QB + 8 * j + 8, :] = jnp.where(low_half, pltpu.roll(a, share, 0), b)


def body(observed, kernel, row_shift, cycle_map, cycle_blocks, chi_map):
    vmem = pl.BlockSpec(memory_space=pltpu.VMEM)
    smem = pl.BlockSpec(memory_space=pltpu.SMEM)
    dma = pltpu.SemaphoreType.DMA
    count = len(OTHERS)
    columns, bands = pl.pallas_call(
        transpose_kernel,
        name="transpose",
        out_shape=(
            jax.ShapeDtypeStruct((TILES, TILE, 2 * BLK), F32),
            jax.ShapeDtypeStruct((TILES, GROUPS, TILE // GROUPS, BLK), F32),
        ),
        in_specs=[vmem, vmem, smem],
        out_specs=(vmem, vmem),
        scratch_shapes=[
            pltpu.VMEM((TILES, TILE, 2 * BLK), F32),
            pltpu.VMEM((TILE // GROUPS, BLK), F32),
            dma((count,)), dma((count,)), dma((count,)), dma((count,)), dma((GROUPS - 1,)), dma((GROUPS - 1,)),
        ],
        compiler_params=pltpu.CompilerParams(collective_id=0, has_side_effects=True, vmem_limit_bytes=VMEM_LIMIT),
    )(observed, kernel, row_shift)

    parts = pl.pallas_call(
        restore_kernel,
        name="restore",
        out_shape=jax.ShapeDtypeStruct((TILES, TILE // 2, BLK), F32),
        in_specs=[vmem, vmem],
        out_specs=vmem,
        scratch_shapes=[
            pltpu.VMEM((PADDED, BLK), F32),
            pltpu.VMEM((KBLKS, 2 * BLK, 2 * BLK), BF16),
            pltpu.VMEM((KBLKS, 2 * BLK, 2 * BLK), BF16),
            pltpu.VMEM((ROWS, 2 * BLK), F32),
        ]
        + [pltpu.VMEM((PADDED, 2 * BLK), BF16)] * 4,
        compiler_params=pltpu.CompilerParams(vmem_limit_bytes=VMEM_LIMIT),
    )(columns.reshape(ROWS, 2 * BLK), bands.reshape(ROWS, BLK))

    return pl.pallas_call(
        bin_kernel,
        name="bin",
        out_shape=jax.ShapeDtypeStruct((TILE, CHI), F32),
        in_specs=[vmem, vmem, smem, pl.BlockSpec(memory_space=pl.ANY)],
        out_specs=vmem,
        scratch_shapes=[
            pltpu.VMEM((CHI, COLS), BF16),
            pltpu.VMEM((TILES, TILE // 2, BLK), F32),
            pltpu.VMEM((TILE, COLS), F32),
            pltpu.VMEM((NC, NX, QB, CHI), F32),
            pltpu.VMEM((NX, QB, CHI), F32),
            pltpu.VMEM((NX, QB, CHI), F32),
            pltpu.VMEM((NX - 1, QB, CHI), F32),
            pltpu.VMEM((QB, CHIP), F32),
            pltpu.VMEM((NY, QB, CHIP), F32),
            pltpu.VMEM((NZ, 8, CHI), F32),
            pltpu.VMEM((NZ - 1, 8, CHI), F32),
            pltpu.VMEM((8, CHI), F32),
            pltpu.VMEM((GROUPS, 8, CHI), F32),
            dma, dma((count,)), dma((count,)), dma, dma,
            dma((NX - 1,)), dma((NX - 1,)), dma((NY - 1,)), dma((NY - 1,)),
            dma((NZ - 1,)), dma((NZ - 1,)), dma((GROUPS - 1,)), dma((GROUPS - 1,)),
        ],
        compiler_params=pltpu.CompilerParams(collective_id=1, has_side_effects=True, vmem_limit_bytes=VMEM_LIMIT),
    )(parts, cycle_map, cycle_blocks, jnp.swapaxes(chi_map, 1, 2))


def solution(mesh):
    return jax.shard_map(
        body,
        mesh=mesh,
        in_specs=(
            P("frames", "rows", None),
            P("rows", None),
            P("rows"),
            P("rows", None),
            P("rows", None),
            P("rows", None, None),
        ),
        out_specs=P("rows", None),
        check_vma=False,
    )
```

```python
import functools

import jax
import jax.numpy as jnp
from jax import lax
from jax.experimental import pallas as pl
from jax.experimental.pallas import tpu as pltpu
from jax.sharding import PartitionSpec as P

NY, NZ, NX, NC = 4, 8, 4, 2
TILES, GROUPS = NY * NZ, NX * NC
ROWS, COLS, TILE = 2048, 2048, 64
F_DEV, BAND, SHIFT, ITERS = 4, 65, 8, 4
REACH = (BAND - 1) // 2 + SHIFT
CHI, QB, NB = 720, 32, 8
BLK = 128
FRONT = 48
PADDED = ROWS + 2 * BLK - BLK
KBLKS = ROWS // BLK
GROUP = 4
CHIP = 768

F32, BF16 = jnp.float32, jnp.bfloat16
MESH = pl.DeviceIdType.MESH
VMEM_LIMIT = 60 * 1024 * 1024

OTHERS = [(dy, dz) for dz in (4, -3, 3, -2, 2, -1, 1, 0) for dy in (2, 1, -1, 0) if (dy, dz) != (0, 0)]


def position():
    group = lax.axis_index("frames")
    tile = lax.axis_index("rows")
    return group, tile, tile // NZ, lax.rem(tile, NZ)


def other_tile(y, z, offset):
    return lax.rem(y + offset[0] + NY, NY) * NZ + lax.rem(z + offset[1] + NZ, NZ)


def greet(group, y, z):
    barrier = pltpu.get_barrier_semaphore()
    for offset in OTHERS:
        pl.semaphore_signal(barrier, inc=1, device_id={"rows": other_tile(y, z, offset)}, device_id_type=MESH)
    for step in range(1, GROUPS):
        pl.semaphore_signal(barrier, inc=1, device_id={"frames": lax.rem(group + step, GROUPS)}, device_id_type=MESH)
    return barrier, len(OTHERS) + GROUPS - 1


def lanes(shape):
    return lax.broadcasted_iota(jnp.int32, shape, len(shape) - 1)


def sublanes(shape):
    return lax.broadcasted_iota(jnp.int32, shape, len(shape) - 2)


def halves(value):
    high = value.astype(BF16)
    return high, (value - high.astype(F32)).astype(BF16)


def remote(src, dst, send_sem, recv_sem, device):
    return pltpu.make_async_remote_copy(
        src_ref=src, dst_ref=dst, send_sem=send_sem, recv_sem=recv_sem, device_id=device, device_id_type=MESH
    )


def program_kernel(
    obs, kern, shift, cyc, ids, chi_hbm, out, packed_0, packed_1, columns_0, columns_1, bands, taps, wide, fwd, adj, est, kept,
    est_hl, rat_hl, weights, parts, chi, got, summed, shared, from_core, mixed, from_x, named, around, placed, from_z, own, final,
    chi_sem, send_0, recv_0, send_1, recv_1, send_t, recv_t, send_f, recv_f,
    send_a, recv_a, send_c, recv_c, send_x, recv_x, send_y, recv_y, send_z, recv_z, send_g, recv_g,
):
    group, tile, y, z = position()
    x, core = group // NC, lax.rem(group, NC)
    load = pltpu.make_async_copy(chi_hbm.at[0], chi, chi_sem)
    load.start()
    barrier, greeted = greet(group, y, z)
    per = TILE // GROUPS

    taps[...] = jnp.zeros_like(taps)
    taps[:, :BAND] = kern[pl.ds(pl.multiple_of(group * per, per), per), :]
    rows_of = sublanes((per, BLK))
    moves = jnp.zeros((per, BLK), jnp.int32)
    for r in range(per):
        moves = jnp.where(rows_of == r, shift[group * per + r] + SHIFT, moves)
    plain = taps[...]
    moved = jnp.zeros((per, BLK), F32)
    for s in range(2 * SHIFT + 1):
        moved = jnp.where(moves == s, pltpu.roll(plain, s, 1) if s else plain, moved)
    target = tile * TILE + group * per + rows_of + lanes((per, BLK)) - REACH
    moved = jnp.where((target >= 0) & (target < ROWS), moved, 0.0)
    bands[tile, group] = moved

    def pack(pair, packed, columns):
        left = lanes((TILE, BLK)) < BLK // 2

        @pl.loop(0, COLS // BLK)
        def _(m):
            a, b = [obs[2 * pair + f, :, pl.ds(pl.multiple_of(m * BLK, BLK), BLK)] for f in range(2)]
            packed[2 * m] = jnp.where(left, a, pltpu.roll(b, BLK // 2, 1))
            packed[2 * m + 1] = jnp.where(left, pltpu.roll(a, BLK // 2, 1), b)

        columns[tile] = packed[tile]

    def exchange(packed, columns, send, recv):
        started = []
        for n, offset in enumerate(OTHERS):
            to = other_tile(y, z, offset)
            copy = remote(packed.at[to], columns.at[tile], send.at[n], recv.at[n], {"rows": to})
            copy.start()
            started.append(copy)
        return started

    pack(0, packed_0, columns_0)
    pl.semaphore_wait(barrier, greeted)
    first = []
    for n, offset in enumerate(OTHERS):
        copy = remote(bands.at[tile, group], bands.at[tile, group], send_t.at[n], recv_t.at[n], {"rows": other_tile(y, z, offset)})
        copy.start()
        first.append(copy)
    pair_0 = exchange(packed_0, columns_0, send_0, recv_0)
    pack(1, packed_1, columns_1)
    pair_1 = exchange(packed_1, columns_1, send_1, recv_1)
    for copy in first:
        copy.wait()
    shares = []
    for step in range(1, GROUPS):
        to = lax.rem(group + step, GROUPS)
        copy = remote(bands.at[:, group], bands.at[:, group], send_f.at[step - 1], recv_f.at[step - 1], {"frames": to})
        copy.start()
        shares.append(copy)

    share = QB // GROUPS
    q = sublanes((NB * QB, NB * QB))
    wanted = ((q // share) % NB) * QB + (q // QB) * share + q % share
    order = (lanes((NB * QB, NB * QB)) == wanted).astype(BF16)
    turn = functools.partial(lax.dot_general, dimension_numbers=(((1,), (1,)), ((), ())), preferred_element_type=F32)
    high, low = halves(cyc[...])
    high, low = turn(order, high).astype(BF16), turn(order, low).astype(BF16)
    weights[...] = jnp.concatenate([high, high, low], axis=1)

    for ref in (est_hl, rat_hl):
        ref[0:FRONT, :] = jnp.zeros((FRONT, 2 * BLK), BF16)
        ref[FRONT + ROWS :, :] = jnp.zeros((PADDED - FRONT - ROWS, 2 * BLK), BF16)
    wide[0:FRONT, :] = jnp.zeros((FRONT, BLK), F32)
    wide[FRONT + ROWS :, :] = jnp.zeros((PADDED - FRONT - ROWS, BLK), F32)
    for copy in shares:
        copy.wait()

    @pl.loop(0, TILES)
    def _(t):
        wide[pl.ds(pl.multiple_of(t * TILE, TILE) + FRONT, TILE), :] = bands[t].reshape(TILE, BLK)

    @pl.loop(0, KBLKS)
    def _(k):
        row = pl.multiple_of(k * BLK, BLK)
        mine = wide[pl.ds(row + FRONT, BLK), :]
        mine = jnp.concatenate([mine, jnp.zeros_like(mine)], axis=1)
        mine = pltpu.roll(mine, FRONT - REACH, 1, stride=1, stride_axis=0)
        high, low = halves(mine)
        fwd[k, 0:BLK, :] = high
        fwd[k, BLK:, :] = low
        near = wide[pl.ds(row, 2 * BLK), :]
        near = jnp.concatenate([near, jnp.zeros_like(near)], axis=1)
        near = pltpu.roll(near, 2 * BLK - (FRONT + REACH), 1, stride=1, stride_axis=0)[:, :BLK]
        near = near / jnp.sum(near, axis=0, keepdims=True)
        high, low = halves(jnp.transpose(near))
        adj[k, 0:BLK, :] = high
        adj[k, BLK:, :] = low

    def product(mat, k, row, field):
        both = jnp.dot(mat[k], field[pl.ds(row, 2 * BLK), :], preferred_element_type=F32)
        return both[:BLK, :BLK] + (both[BLK:, :BLK] + both[:BLK, BLK:])

    def in_groups(step):
        @pl.loop(0, KBLKS // GROUP)
        def _(g):
            blocks = []
            for j in range(GROUP):
                k = g * GROUP + j
                row = pl.multiple_of(k * BLK, BLK)
                blocks.append((row, step(row, k)))
            for row, store in blocks:
                store(row)

    def store_halves(value, field, row):
        high, low = halves(value)
        field[pl.ds(row + FRONT, BLK), 0:BLK] = high
        field[pl.ds(row + FRONT, BLK), BLK:] = low

    def restore(columns, last_block):
        def seen(k):
            return columns[pl.ds(2 * k, 2)].reshape(BLK, BLK)

        def start_block(row, k):
            value = seen(k)

            def store(row):
                est[pl.ds(row, BLK), :] = value
                store_halves(value, est_hl, row)

            return store

        def forward_block(row, k):
            return functools.partial(store_halves, seen(k) / product(fwd, k, row, est_hl), rat_hl)

        def renewed(row, k):
            return est[pl.ds(row, BLK), :] * product(adj, k, row, rat_hl)

        def adjoint_block(row, k):
            value = renewed(row, k)

            def store(row):
                est[pl.ds(row, BLK), :] = value
                store_halves(value, est_hl, row)

            return store

        in_groups(start_block)

        @pl.loop(0, ITERS - 1)
        def _(repeat):
            in_groups(forward_block)
            in_groups(adjoint_block)

        in_groups(forward_block)
        in_groups(lambda row, k: last_block(row, k, renewed(row, k)))

    left = lanes((TILE // 2, BLK)) < BLK // 2

    def keep_block(row, k, value):
        def store(row):
            kept[pl.ds(row, BLK), :] = value

        return store

    def sum_block(row, k, value):
        value = kept[pl.ds(row, BLK), :] + value
        value = value + pltpu.roll(value, BLK // 2, 1)

        def store(row):
            for half in range(2):
                top = half * TILE
                parts[2 * k + half] = jnp.where(left, value[top : top + TILE // 2], value[top + TILE // 2 : top + TILE])

        return store

    for copy in pair_0:
        copy.wait()
    restore(columns_0, keep_block)
    for copy in pair_1:
        copy.wait()
    restore(columns_1, sum_block)
    got[tile] = parts[tile]

    copies = []
    for n, offset in enumerate(OTHERS):
        to = other_tile(y, z, offset)
        copy = remote(parts.at[to], got.at[tile], send_a.at[n], recv_a.at[n], {"rows": to})
        copy.start()
        copies.append(copy)
    for copy in copies:
        copy.wait()

    for m in range(COLS // BLK):
        a, b = got[2 * m], got[2 * m + 1]
        summed[0 : TILE // 2, m * BLK : (m + 1) * BLK] = jnp.where(left, a, pltpu.roll(b, BLK // 2, 1))
        summed[TILE // 2 :, m * BLK : (m + 1) * BLK] = jnp.where(left, pltpu.roll(a, BLK // 2, 1), b)
    load.wait()
    turn_chi = functools.partial(lax.dot_general, dimension_numbers=(((1,), (1,)), ((), ())), preferred_element_type=F32)
    total = jnp.zeros((NB * QB, CHI), F32)
    step = COLS // 4
    for m in range(4):
        high, low = halves(summed[:, m * step : (m + 1) * step])
        part = jnp.dot(weights[...], jnp.concatenate([high, low, high], axis=0), preferred_element_type=F32).astype(BF16)
        total = total + turn_chi(part, chi[:, m * step : (m + 1) * step])
    for i in range(NX):
        for j in range(NC):
            top = (i * NC + j) * QB
            shared[j, i] = total[top : top + QB]

    swap = remote(shared.at[1 - core], from_core, send_c, recv_c, {"frames": x * NC + 1 - core})
    swap.start()
    swap.wait()
    mixed[...] = shared[core] + from_core[...]
    copies = []
    for n in range(1, NX):
        to = lax.rem(x + n, NX)
        copy = remote(mixed.at[to], from_x.at[n - 1], send_x.at[n - 1], recv_x.at[n - 1], {"frames": to * NC + core})
        copy.start()
        copies.append(copy)
    for copy in copies:
        copy.wait()
    value = mixed[x] + from_x[0] + from_x[1] + from_x[2]

    last = CHIP - BLK
    named[:, 0:last] = value[:, 0:last]
    lane, sub = lanes((QB, BLK)), sublanes((QB, BLK))
    label = jnp.zeros((QB, BLK), jnp.int32)
    for b in range(NB):
        label = jnp.where(sub // share == b, ids[0, b], label)
    tail = jnp.concatenate([value[:, last:], jnp.zeros((QB, CHIP - CHI), F32)], axis=1)
    named[:, last:] = jnp.where(lane == CHI - last, label.astype(F32), tail)
    around[y] = named[...]
    copies = []
    for n in range(1, NY):
        to = lax.rem(y + n, NY) * NZ + z
        copy = remote(named, around.at[y], send_y.at[n - 1], recv_y.at[n - 1], {"rows": to})
        copy.start()
        copies.append(copy)
    for copy in copies:
        copy.wait()

    every = around[...].reshape(NY * QB, CHIP)
    label = every[:, CHI : CHI + 1]
    rows_of, slot = sublanes((NY * QB, NZ * 2 * share)), lanes((NY * QB, NZ * 2 * share))
    owner_block = 2 * (y * NZ) + slot // share
    hit = (label == owner_block.astype(F32)) & (rows_of % share == slot % share)
    hit = hit.astype(BF16)
    high, low = halves(every)
    low2 = (every - high.astype(F32) - low.astype(F32)).astype(BF16)
    place = functools.partial(lax.dot_general, dimension_numbers=(((0,), (0,)), ((), ())), preferred_element_type=F32)
    put = place(jnp.concatenate([hit, hit, hit], axis=0), jnp.concatenate([high, low, low2], axis=0))
    for k in range(NZ):
        placed[k] = put[k * 2 * share : (k + 1) * 2 * share, :CHI]
    copies = []
    for n in range(1, NZ):
        to = lax.rem(z + n, NZ)
        copy = remote(placed.at[to], from_z.at[n - 1], send_z.at[n - 1], recv_z.at[n - 1], {"rows": y * NZ + to})
        copy.start()
        copies.append(copy)
    for copy in copies:
        copy.wait()
    value = placed[z]
    for n in range(NZ - 1):
        value = value + from_z[n]
    own[...] = value
    final[group] = value
    copies = []
    for n in range(1, GROUPS):
        copy = remote(own, final.at[group], send_g.at[n - 1], recv_g.at[n - 1], {"frames": lax.rem(group + n, GROUPS)})
        copy.start()
        copies.append(copy)
    for copy in copies:
        copy.wait()
    low_half = sublanes((2 * share, CHI)) < share
    for j in range(GROUPS // 2):
        a, b = final[2 * j], final[2 * j + 1]
        out[8 * j : 8 * j + 8, :] = jnp.where(low_half, a, pltpu.roll(b, share, 0))
        out[QB + 8 * j : QB + 8 * j + 8, :] = jnp.where(low_half, pltpu.roll(a, share, 0), b)


def body(observed, kernel, row_shift, cycle_map, cycle_blocks, chi_map):
    vmem = pl.BlockSpec(memory_space=pltpu.VMEM)
    smem = pl.BlockSpec(memory_space=pltpu.SMEM)
    dma = pltpu.SemaphoreType.DMA
    count = len(OTHERS)
    return pl.pallas_call(
        program_kernel,
        name="restore_and_bin",
        out_shape=jax.ShapeDtypeStruct((TILE, CHI), F32),
        in_specs=[vmem, vmem, smem, vmem, smem, pl.BlockSpec(memory_space=pl.ANY)],
        out_specs=vmem,
        scratch_shapes=[pltpu.VMEM((TILES, TILE, BLK), F32)] * 4
        + [
            pltpu.VMEM((TILES, GROUPS, TILE // GROUPS, BLK), F32),
            pltpu.VMEM((TILE // GROUPS, BLK), F32),
            pltpu.VMEM((PADDED, BLK), F32),
            pltpu.VMEM((KBLKS, 2 * BLK, 2 * BLK), BF16),
            pltpu.VMEM((KBLKS, 2 * BLK, 2 * BLK), BF16),
            pltpu.VMEM((ROWS, BLK), F32),
            pltpu.VMEM((ROWS, BLK), F32),
            pltpu.VMEM((PADDED, 2 * BLK), BF16),
            pltpu.VMEM((PADDED, 2 * BLK), BF16),
            pltpu.VMEM((NB * QB, 3 * TILE), BF16),
            pltpu.VMEM((TILES, TILE // 2, BLK), F32),
            pltpu.VMEM((CHI, COLS), BF16),
            pltpu.VMEM((TILES, TILE // 2, BLK), F32),
            pltpu.VMEM((TILE, COLS), F32),
            pltpu.VMEM((NC, NX, QB, CHI), F32),
            pltpu.VMEM((NX, QB, CHI), F32),
            pltpu.VMEM((NX, QB, CHI), F32),
            pltpu.VMEM((NX - 1, QB, CHI), F32),
            pltpu.VMEM((QB, CHIP), F32),
            pltpu.VMEM((NY, QB, CHIP), F32),
            pltpu.VMEM((NZ, 8, CHI), F32),
            pltpu.VMEM((NZ - 1, 8, CHI), F32),
            pltpu.VMEM((8, CHI), F32),
            pltpu.VMEM((GROUPS, 8, CHI), F32),
            dma,
            dma((count,)), dma((count,)), dma((count,)), dma((count,)),
            dma((count,)), dma((count,)), dma((GROUPS - 1,)), dma((GROUPS - 1,)),
            dma((count,)), dma((count,)), dma, dma,
            dma((NX - 1,)), dma((NX - 1,)), dma((NY - 1,)), dma((NY - 1,)),
            dma((NZ - 1,)), dma((NZ - 1,)), dma((GROUPS - 1,)), dma((GROUPS - 1,)),
        ],
        compiler_params=pltpu.CompilerParams(collective_id=0, has_side_effects=True, vmem_limit_bytes=VMEM_LIMIT),
    )(observed, kernel, row_shift, cycle_map, cycle_blocks, jnp.swapaxes(chi_map, 1, 2))


def solution(mesh):
    return jax.shard_map(
        body,
        mesh=mesh,
        in_specs=(
            P("frames", "rows", None),
            P("rows", None),
            P("rows"),
            P("rows", None),
            P("rows", None),
            P("rows", None, None),
        ),
        out_specs=P("rows", None),
        check_vma=False,
    )
```

```python
import functools

import jax
import jax.numpy as jnp
from jax import lax
from jax.experimental import pallas as pl
from jax.experimental.pallas import tpu as pltpu
from jax.sharding import PartitionSpec as P

NY, NZ, NX, NC = 4, 8, 4, 2
TILES, GROUPS = NY * NZ, NX * NC
ROWS, COLS, TILE = 2048, 2048, 64
F_DEV, BAND, SHIFT, ITERS = 4, 65, 8, 4
REACH = (BAND - 1) // 2 + SHIFT
CHI, QB, NB = 720, 32, 8
BLK = 128
FRONT = 48
PADDED = ROWS + 2 * BLK - BLK
KBLKS = ROWS // BLK
GROUP = 4
PIECE = 32
CHIP = 768

F32, BF16 = jnp.float32, jnp.bfloat16
MESH = pl.DeviceIdType.MESH
VMEM_LIMIT = 60 * 1024 * 1024

OTHERS = [(dy, dz) for dz in (4, -3, 3, -2, 2, -1, 1, 0) for dy in (2, 1, -1, 0) if (dy, dz) != (0, 0)]


def position():
    group = lax.axis_index("frames")
    tile = lax.axis_index("rows")
    return group, tile, tile // NZ, lax.rem(tile, NZ)


def other_tile(y, z, offset):
    return lax.rem(y + offset[0] + NY, NY) * NZ + lax.rem(z + offset[1] + NZ, NZ)


def greet(group, y, z):
    barrier = pltpu.get_barrier_semaphore()
    for offset in OTHERS:
        pl.semaphore_signal(barrier, inc=1, device_id={"rows": other_tile(y, z, offset)}, device_id_type=MESH)
    for step in range(1, GROUPS):
        pl.semaphore_signal(barrier, inc=1, device_id={"frames": lax.rem(group + step, GROUPS)}, device_id_type=MESH)
    return barrier, len(OTHERS) + GROUPS - 1


def lanes(shape):
    return lax.broadcasted_iota(jnp.int32, shape, len(shape) - 1)


def sublanes(shape):
    return lax.broadcasted_iota(jnp.int32, shape, len(shape) - 2)


def halves(value):
    high = value.astype(BF16)
    return high, (value - high.astype(F32)).astype(BF16)


def interleave(blocks, i, lane_group):
    result = blocks[i]
    for j in range(len(blocks)):
        if j != i:
            result = jnp.where(lane_group == j, pltpu.roll(blocks[j], PIECE * (j - i) % BLK, 1), result)
    return result


def remote(src, dst, send_sem, recv_sem, device):
    return pltpu.make_async_remote_copy(
        src_ref=src, dst_ref=dst, send_sem=send_sem, recv_sem=recv_sem, device_id=device, device_id_type=MESH
    )


def program_kernel(
    obs, kern, shift, cyc, ids, chi_hbm, out, packed_0, packed_1, columns_0, columns_1, bands, taps, wide, fwd, adj, est,
    est_hl, rat_hl, weights, parts_0, parts_1, got_0, got_1, chi, summed, shared, from_core, mixed, from_x, named, around, placed, from_z, own, final,
    chi_sem, send_0, recv_0, send_1, recv_1, send_t, recv_t, send_f, recv_f,
    send_a, recv_a, send_b, recv_b, send_c, recv_c, send_x, recv_x, send_y, recv_y, send_z, recv_z, send_g, recv_g,
):
    group, tile, y, z = position()
    x, core = group // NC, lax.rem(group, NC)
    load = pltpu.make_async_copy(chi_hbm.at[0], chi, chi_sem)
    load.start()
    barrier, greeted = greet(group, y, z)
    per = TILE // GROUPS

    taps[...] = jnp.zeros_like(taps)
    taps[:, :BAND] = kern[pl.ds(pl.multiple_of(group * per, per), per), :]
    rows_of = sublanes((per, BLK))
    moves = jnp.zeros((per, BLK), jnp.int32)
    for r in range(per):
        moves = jnp.where(rows_of == r, shift[group * per + r] + SHIFT, moves)
    plain = taps[...]
    moved = jnp.zeros((per, BLK), F32)
    for s in range(2 * SHIFT + 1):
        moved = jnp.where(moves == s, pltpu.roll(plain, s, 1) if s else plain, moved)
    target = tile * TILE + group * per + rows_of + lanes((per, BLK)) - REACH
    moved = jnp.where((target >= 0) & (target < ROWS), moved, 0.0)
    bands[tile, group] = moved

    lane_group = lanes((TILE, BLK)) // PIECE

    def pack(half, packed, columns):
        @pl.loop(0, COLS // BLK // 2)
        def _(m):
            first_lane = pl.multiple_of((half * (COLS // BLK // 2) + m) * BLK, BLK)
            frames = [obs[f, :, pl.ds(first_lane, BLK)] for f in range(F_DEV)]
            for i in range(F_DEV):
                packed[F_DEV * m + i] = interleave(frames, i, lane_group)

        columns[tile] = packed[tile]

    def exchange(packed, columns, send, recv):
        started = []
        for n, offset in enumerate(OTHERS):
            to = other_tile(y, z, offset)
            copy = remote(packed.at[to], columns.at[tile], send.at[n], recv.at[n], {"rows": to})
            copy.start()
            started.append(copy)
        return started

    pack(0, packed_0, columns_0)
    pl.semaphore_wait(barrier, greeted)
    first = []
    for n, offset in enumerate(OTHERS):
        copy = remote(bands.at[tile, group], bands.at[tile, group], send_t.at[n], recv_t.at[n], {"rows": other_tile(y, z, offset)})
        copy.start()
        first.append(copy)
    half_0 = exchange(packed_0, columns_0, send_0, recv_0)
    pack(1, packed_1, columns_1)
    half_1 = exchange(packed_1, columns_1, send_1, recv_1)
    for copy in first:
        copy.wait()
    shares = []
    for step in range(1, GROUPS):
        to = lax.rem(group + step, GROUPS)
        copy = remote(bands.at[:, group], bands.at[:, group], send_f.at[step - 1], recv_f.at[step - 1], {"frames": to})
        copy.start()
        shares.append(copy)

    share = QB // GROUPS
    q = sublanes((NB * QB, NB * QB))
    wanted = ((q // share) % NB) * QB + (q // QB) * share + q % share
    order = (lanes((NB * QB, NB * QB)) == wanted).astype(BF16)
    turn = functools.partial(lax.dot_general, dimension_numbers=(((1,), (1,)), ((), ())), preferred_element_type=F32)
    high, low = halves(cyc[...])
    high, low = turn(order, high).astype(BF16), turn(order, low).astype(BF16)
    weights[...] = jnp.concatenate([high, high, low], axis=1)

    for ref in (est_hl, rat_hl):
        ref[0:FRONT, :] = jnp.zeros((FRONT, 2 * BLK), BF16)
        ref[FRONT + ROWS :, :] = jnp.zeros((PADDED - FRONT - ROWS, 2 * BLK), BF16)
    wide[0:FRONT, :] = jnp.zeros((FRONT, BLK), F32)
    wide[FRONT + ROWS :, :] = jnp.zeros((PADDED - FRONT - ROWS, BLK), F32)
    for copy in shares:
        copy.wait()

    @pl.loop(0, TILES)
    def _(t):
        wide[pl.ds(pl.multiple_of(t * TILE, TILE) + FRONT, TILE), :] = bands[t].reshape(TILE, BLK)

    @pl.loop(0, KBLKS)
    def _(k):
        row = pl.multiple_of(k * BLK, BLK)
        mine = wide[pl.ds(row + FRONT, BLK), :]
        mine = jnp.concatenate([mine, jnp.zeros_like(mine)], axis=1)
        mine = pltpu.roll(mine, FRONT - REACH, 1, stride=1, stride_axis=0)
        high, low = halves(mine)
        fwd[k, 0:BLK, :] = high
        fwd[k, BLK:, :] = low
        near = wide[pl.ds(row, 2 * BLK), :]
        near = jnp.concatenate([near, jnp.zeros_like(near)], axis=1)
        near = pltpu.roll(near, 2 * BLK - (FRONT + REACH), 1, stride=1, stride_axis=0)[:, :BLK]
        near = near / jnp.sum(near, axis=0, keepdims=True)
        high, low = halves(jnp.transpose(near))
        adj[k, 0:BLK, :] = high
        adj[k, BLK:, :] = low

    def product(mat, k, row, field):
        both = jnp.dot(mat[k], field[pl.ds(row, 2 * BLK), :], preferred_element_type=F32)
        return both[:BLK, :BLK] + (both[BLK:, :BLK] + both[:BLK, BLK:])

    def in_groups(step):
        @pl.loop(0, KBLKS // GROUP)
        def _(g):
            blocks = []
            for j in range(GROUP):
                k = g * GROUP + j
                row = pl.multiple_of(k * BLK, BLK)
                blocks.append((row, step(row, k)))
            for row, store in blocks:
                store(row)

    def store_halves(value, field, row):
        high, low = halves(value)
        field[pl.ds(row + FRONT, BLK), 0:BLK] = high
        field[pl.ds(row + FRONT, BLK), BLK:] = low

    def restore(columns, last_block):
        def seen(k):
            return columns[pl.ds(2 * k, 2)].reshape(BLK, BLK)

        def start_block(row, k):
            value = seen(k)

            def store(row):
                est[pl.ds(row, BLK), :] = value
                store_halves(value, est_hl, row)

            return store

        def forward_block(row, k):
            return functools.partial(store_halves, seen(k) / product(fwd, k, row, est_hl), rat_hl)

        def renewed(row, k):
            return est[pl.ds(row, BLK), :] * product(adj, k, row, rat_hl)

        def adjoint_block(row, k):
            value = renewed(row, k)

            def store(row):
                est[pl.ds(row, BLK), :] = value
                store_halves(value, est_hl, row)

            return store

        in_groups(start_block)

        @pl.loop(0, ITERS - 1)
        def _(repeat):
            in_groups(forward_block)
            in_groups(adjoint_block)

        in_groups(forward_block)
        in_groups(lambda row, k: last_block(row, k, renewed(row, k)))

    quarter = TILE // F_DEV
    quarter_group = lanes((quarter, BLK)) // PIECE

    def sum_into(parts):
        def sum_block(row, k, value):
            value = value + pltpu.roll(value, BLK // 2, 1)
            value = value + pltpu.roll(value, BLK // 4, 1)

            def store(row):
                for top in range(2):
                    rows = [value[top * TILE + i * quarter : top * TILE + (i + 1) * quarter] for i in range(F_DEV)]
                    result = rows[0]
                    for i in range(1, F_DEV):
                        result = jnp.where(quarter_group == i, rows[i], result)
                    parts[2 * k + top] = result

            return store

        return sum_block

    def bin_half(half, got, total):
        for m in range(COLS // BLK // 2):
            blocks = [got[F_DEV * m + j] for j in range(F_DEV)]
            for i in range(F_DEV):
                summed[i * quarter : (i + 1) * quarter, m * BLK : (m + 1) * BLK] = interleave(blocks, i, quarter_group)
        step = COLS // 4
        for m in range(2):
            high, low = halves(summed[:, m * step : (m + 1) * step])
            part = jnp.dot(weights[...], jnp.concatenate([high, low, high], axis=0), preferred_element_type=F32).astype(BF16)
            total = total + turn(part, chi[:, (2 * half + m) * step : (2 * half + m + 1) * step])
        return total

    for copy in half_0:
        copy.wait()
    restore(columns_0, sum_into(parts_0))
    got_0[tile] = parts_0[tile]
    back_0 = exchange(parts_0, got_0, send_a, recv_a)
    for copy in half_1:
        copy.wait()
    restore(columns_1, sum_into(parts_1))
    got_1[tile] = parts_1[tile]
    back_1 = exchange(parts_1, got_1, send_b, recv_b)
    for copy in back_0:
        copy.wait()
    load.wait()
    total = bin_half(0, got_0, jnp.zeros((NB * QB, CHI), F32))
    for copy in back_1:
        copy.wait()
    total = bin_half(1, got_1, total)
    for i in range(NX):
        for j in range(NC):
            top = (i * NC + j) * QB
            shared[j, i] = total[top : top + QB]

    swap = remote(shared.at[1 - core], from_core, send_c, recv_c, {"frames": x * NC + 1 - core})
    swap.start()
    swap.wait()
    mixed[...] = shared[core] + from_core[...]
    copies = []
    for n in range(1, NX):
        to = lax.rem(x + n, NX)
        copy = remote(mixed.at[to], from_x.at[n - 1], send_x.at[n - 1], recv_x.at[n - 1], {"frames": to * NC + core})
        copy.start()
        copies.append(copy)
    for copy in copies:
        copy.wait()
    value = mixed[x] + from_x[0] + from_x[1] + from_x[2]

    last = CHIP - BLK
    named[:, 0:last] = value[:, 0:last]
    lane, sub = lanes((QB, BLK)), sublanes((QB, BLK))
    label = jnp.zeros((QB, BLK), jnp.int32)
    for b in range(NB):
        label = jnp.where(sub // share == b, ids[0, b], label)
    tail = jnp.concatenate([value[:, last:], jnp.zeros((QB, CHIP - CHI), F32)], axis=1)
    named[:, last:] = jnp.where(lane == CHI - last, label.astype(F32), tail)
    around[y] = named[...]
    copies = []
    for n in range(1, NY):
        to = lax.rem(y + n, NY) * NZ + z
        copy = remote(named, around.at[y], send_y.at[n - 1], recv_y.at[n - 1], {"rows": to})
        copy.start()
        copies.append(copy)
    for copy in copies:
        copy.wait()

    every = around[...].reshape(NY * QB, CHIP)
    label = every[:, CHI : CHI + 1]
    rows_of, slot = sublanes((NY * QB, NZ * 2 * share)), lanes((NY * QB, NZ * 2 * share))
    owner_block = 2 * (y * NZ) + slot // share
    hit = (label == owner_block.astype(F32)) & (rows_of % share == slot % share)
    hit = hit.astype(BF16)
    high, low = halves(every)
    low2 = (every - high.astype(F32) - low.astype(F32)).astype(BF16)
    place = functools.partial(lax.dot_general, dimension_numbers=(((0,), (0,)), ((), ())), preferred_element_type=F32)
    put = place(jnp.concatenate([hit, hit, hit], axis=0), jnp.concatenate([high, low, low2], axis=0))
    for k in range(NZ):
        placed[k] = put[k * 2 * share : (k + 1) * 2 * share, :CHI]
    copies = []
    for n in range(1, NZ):
        to = lax.rem(z + n, NZ)
        copy = remote(placed.at[to], from_z.at[n - 1], send_z.at[n - 1], recv_z.at[n - 1], {"rows": y * NZ + to})
        copy.start()
        copies.append(copy)
    for copy in copies:
        copy.wait()
    value = placed[z]
    for n in range(NZ - 1):
        value = value + from_z[n]
    own[...] = value
    final[group] = value
    copies = []
    for n in range(1, GROUPS):
        copy = remote(own, final.at[group], send_g.at[n - 1], recv_g.at[n - 1], {"frames": lax.rem(group + n, GROUPS)})
        copy.start()
        copies.append(copy)
    for copy in copies:
        copy.wait()
    low_half = sublanes((2 * share, CHI)) < share
    for j in range(GROUPS // 2):
        a, b = final[2 * j], final[2 * j + 1]
        out[8 * j : 8 * j + 8, :] = jnp.where(low_half, a, pltpu.roll(b, share, 0))
        out[QB + 8 * j : QB + 8 * j + 8, :] = jnp.where(low_half, pltpu.roll(a, share, 0), b)


def body(observed, kernel, row_shift, cycle_map, cycle_blocks, chi_map):
    vmem = pl.BlockSpec(memory_space=pltpu.VMEM)
    smem = pl.BlockSpec(memory_space=pltpu.SMEM)
    dma = pltpu.SemaphoreType.DMA
    count = len(OTHERS)
    return pl.pallas_call(
        program_kernel,
        name="restore_and_bin",
        out_shape=jax.ShapeDtypeStruct((TILE, CHI), F32),
        in_specs=[vmem, vmem, smem, vmem, smem, pl.BlockSpec(memory_space=pl.ANY)],
        out_specs=vmem,
        scratch_shapes=[pltpu.VMEM((TILES, TILE, BLK), F32)] * 4
        + [
            pltpu.VMEM((TILES, GROUPS, TILE // GROUPS, BLK), F32),
            pltpu.VMEM((TILE // GROUPS, BLK), F32),
            pltpu.VMEM((PADDED, BLK), F32),
            pltpu.VMEM((KBLKS, 2 * BLK, 2 * BLK), BF16),
            pltpu.VMEM((KBLKS, 2 * BLK, 2 * BLK), BF16),
            pltpu.VMEM((ROWS, BLK), F32),
            pltpu.VMEM((PADDED, 2 * BLK), BF16),
            pltpu.VMEM((PADDED, 2 * BLK), BF16),
            pltpu.VMEM((NB * QB, 3 * TILE), BF16),
        ]
        + [pltpu.VMEM((TILES, TILE // F_DEV, BLK), F32)] * 4
        + [
            pltpu.VMEM((CHI, COLS), BF16),
            pltpu.VMEM((TILE, COLS // 2), F32),
            pltpu.VMEM((NC, NX, QB, CHI), F32),
            pltpu.VMEM((NX, QB, CHI), F32),
            pltpu.VMEM((NX, QB, CHI), F32),
            pltpu.VMEM((NX - 1, QB, CHI), F32),
            pltpu.VMEM((QB, CHIP), F32),
            pltpu.VMEM((NY, QB, CHIP), F32),
            pltpu.VMEM((NZ, 8, CHI), F32),
            pltpu.VMEM((NZ - 1, 8, CHI), F32),
            pltpu.VMEM((8, CHI), F32),
            pltpu.VMEM((GROUPS, 8, CHI), F32),
            dma,
            dma((count,)), dma((count,)), dma((count,)), dma((count,)),
            dma((count,)), dma((count,)), dma((GROUPS - 1,)), dma((GROUPS - 1,)),
            dma((count,)), dma((count,)), dma((count,)), dma((count,)), dma, dma,
            dma((NX - 1,)), dma((NX - 1,)), dma((NY - 1,)), dma((NY - 1,)),
            dma((NZ - 1,)), dma((NZ - 1,)), dma((GROUPS - 1,)), dma((GROUPS - 1,)),
        ],
        compiler_params=pltpu.CompilerParams(collective_id=0, has_side_effects=True, vmem_limit_bytes=VMEM_LIMIT),
    )(observed, kernel, row_shift, cycle_map, cycle_blocks, jnp.swapaxes(chi_map, 1, 2))


def solution(mesh):
    return jax.shard_map(
        body,
        mesh=mesh,
        in_specs=(
            P("frames", "rows", None),
            P("rows", None),
            P("rows"),
            P("rows", None),
            P("rows", None),
            P("rows", None, None),
        ),
        out_specs=P("rows", None),
        check_vma=False,
    )
```

```python
import functools

import jax
import jax.numpy as jnp
from jax import lax
from jax.experimental import pallas as pl
from jax.experimental.pallas import tpu as pltpu
from jax.sharding import PartitionSpec as P

NY, NZ, NX, NC = 4, 8, 4, 2
TILES, GROUPS = NY * NZ, NX * NC
ROWS, COLS, TILE = 2048, 2048, 64
F_DEV, BAND, SHIFT, ITERS = 4, 65, 8, 4
REACH = (BAND - 1) // 2 + SHIFT
CHI, QB, NB = 720, 32, 8
BLK = 128
FRONT = 48
PADDED = ROWS + 2 * BLK - BLK
KBLKS = ROWS // BLK
GROUP = 4
PIECE = 32
BINS = ((0, 384), (384, CHI))

F32, BF16 = jnp.float32, jnp.bfloat16
MESH = pl.DeviceIdType.MESH
VMEM_LIMIT = 60 * 1024 * 1024

OTHERS = [(dy, dz) for dz in (4, -3, 3, -2, 2, -1, 1, 0) for dy in (2, 1, -1, 0) if (dy, dz) != (0, 0)]


def position():
    group = lax.axis_index("frames")
    tile = lax.axis_index("rows")
    return group, tile, tile // NZ, lax.rem(tile, NZ)


def other_tile(y, z, offset):
    return lax.rem(y + offset[0] + NY, NY) * NZ + lax.rem(z + offset[1] + NZ, NZ)


def greet(group, y, z):
    barrier = pltpu.get_barrier_semaphore()
    for offset in OTHERS:
        pl.semaphore_signal(barrier, inc=1, device_id={"rows": other_tile(y, z, offset)}, device_id_type=MESH)
    for step in range(1, GROUPS):
        pl.semaphore_signal(barrier, inc=1, device_id={"frames": lax.rem(group + step, GROUPS)}, device_id_type=MESH)
    return barrier, len(OTHERS) + GROUPS - 1


def lanes(shape):
    return lax.broadcasted_iota(jnp.int32, shape, len(shape) - 1)


def sublanes(shape):
    return lax.broadcasted_iota(jnp.int32, shape, len(shape) - 2)


def halves(value):
    high = value.astype(BF16)
    return high, (value - high.astype(F32)).astype(BF16)


def interleave(blocks, i, lane_group):
    result = blocks[i]
    for j in range(len(blocks)):
        if j != i:
            result = jnp.where(lane_group == j, pltpu.roll(blocks[j], PIECE * (j - i) % BLK, 1), result)
    return result


def remote(src, dst, send_sem, recv_sem, device):
    return pltpu.make_async_remote_copy(
        src_ref=src, dst_ref=dst, send_sem=send_sem, recv_sem=recv_sem, device_id=device, device_id_type=MESH
    )


def program_kernel(
    obs, kern, shift, cyc, ids, chi_hbm, out, packed_0, packed_1, columns_0, columns_1, bands, taps, wide, fwd, adj, est,
    est_hl, rat_hl, weights, parts_0, parts_1, got_0, got_1, chi, summed, cycles, labels, hits, *rest,
):
    chunks, sems = rest[: 9 * len(BINS)], rest[9 * len(BINS) :]
    (
        chi_sem, send_0, recv_0, send_1, recv_1, send_t, recv_t, send_f, recv_f, send_l, recv_l, send_a, recv_a, send_b, recv_b,
        send_c, recv_c, send_x, recv_x, send_y, recv_y, send_z, recv_z, send_g, recv_g,
    ) = sems
    group, tile, y, z = position()
    x, core = group // NC, lax.rem(group, NC)
    load = pltpu.make_async_copy(chi_hbm.at[0], chi, chi_sem)
    load.start()
    barrier, greeted = greet(group, y, z)
    per = TILE // GROUPS

    taps[...] = jnp.zeros_like(taps)
    taps[:, :BAND] = kern[pl.ds(pl.multiple_of(group * per, per), per), :]
    rows_of = sublanes((per, BLK))
    moves = jnp.zeros((per, BLK), jnp.int32)
    for r in range(per):
        moves = jnp.where(rows_of == r, shift[group * per + r] + SHIFT, moves)
    plain = taps[...]
    moved = jnp.zeros((per, BLK), F32)
    for s in range(2 * SHIFT + 1):
        moved = jnp.where(moves == s, pltpu.roll(plain, s, 1) if s else plain, moved)
    target = tile * TILE + group * per + rows_of + lanes((per, BLK)) - REACH
    moved = jnp.where((target >= 0) & (target < ROWS), moved, 0.0)
    bands[tile, group] = moved

    lane_group = lanes((TILE, BLK)) // PIECE

    def pack(half, packed, columns):
        @pl.loop(0, COLS // BLK // 2)
        def _(m):
            first_lane = pl.multiple_of((half * (COLS // BLK // 2) + m) * BLK, BLK)
            frames = [obs[f, :, pl.ds(first_lane, BLK)] for f in range(F_DEV)]
            for i in range(F_DEV):
                packed[F_DEV * m + i] = interleave(frames, i, lane_group)

        columns[tile] = packed[tile]

    def exchange(packed, columns, send, recv):
        started = []
        for n, offset in enumerate(OTHERS):
            to = other_tile(y, z, offset)
            copy = remote(packed.at[to], columns.at[tile], send.at[n], recv.at[n], {"rows": to})
            copy.start()
            started.append(copy)
        return started

    share = QB // GROUPS
    sub = sublanes((QB, BLK))
    label = jnp.zeros((QB, BLK), jnp.int32)
    for b in range(NB):
        label = jnp.where(sub // share == b, ids[0, b], label)
    labels[y] = label.astype(F32)

    pack(0, packed_0, columns_0)
    pl.semaphore_wait(barrier, greeted)
    first = []
    for n, offset in enumerate(OTHERS):
        copy = remote(bands.at[tile, group], bands.at[tile, group], send_t.at[n], recv_t.at[n], {"rows": other_tile(y, z, offset)})
        copy.start()
        first.append(copy)
    for n in range(1, NY):
        to = lax.rem(y + n, NY) * NZ + z
        copy = remote(labels.at[y], labels.at[y], send_l.at[n - 1], recv_l.at[n - 1], {"rows": to})
        copy.start()
        first.append(copy)
    half_0 = exchange(packed_0, columns_0, send_0, recv_0)
    pack(1, packed_1, columns_1)
    half_1 = exchange(packed_1, columns_1, send_1, recv_1)
    for copy in first:
        copy.wait()
    shares = []
    for step in range(1, GROUPS):
        to = lax.rem(group + step, GROUPS)
        copy = remote(bands.at[:, group], bands.at[:, group], send_f.at[step - 1], recv_f.at[step - 1], {"frames": to})
        copy.start()
        shares.append(copy)

    q = sublanes((NB * QB, NB * QB))
    wanted = ((q // share) % NB) * QB + (q // QB) * share + q % share
    order = (lanes((NB * QB, NB * QB)) == wanted).astype(BF16)
    turn = functools.partial(lax.dot_general, dimension_numbers=(((1,), (1,)), ((), ())), preferred_element_type=F32)
    high, low = halves(cyc[...])
    high, low = turn(order, high).astype(BF16), turn(order, low).astype(BF16)
    weights[...] = jnp.concatenate([high, high, low], axis=1)

    rows_of, slot = sublanes((NY * QB, BLK)), lanes((NY * QB, BLK))
    owner_block = 2 * (y * NZ) + slot // share
    hit = (labels[...].reshape(NY * QB, BLK) == owner_block.astype(F32)) & (rows_of % share == slot % share)
    hits[...] = hit.astype(BF16)[:, : NZ * 2 * share]

    for ref in (est_hl, rat_hl):
        ref[0:FRONT, :] = jnp.zeros((FRONT, 2 * BLK), BF16)
        ref[FRONT + ROWS :, :] = jnp.zeros((PADDED - FRONT - ROWS, 2 * BLK), BF16)
    wide[0:FRONT, :] = jnp.zeros((FRONT, BLK), F32)
    wide[FRONT + ROWS :, :] = jnp.zeros((PADDED - FRONT - ROWS, BLK), F32)
    for copy in shares:
        copy.wait()

    @pl.loop(0, TILES)
    def _(t):
        wide[pl.ds(pl.multiple_of(t * TILE, TILE) + FRONT, TILE), :] = bands[t].reshape(TILE, BLK)

    @pl.loop(0, KBLKS)
    def _(k):
        row = pl.multiple_of(k * BLK, BLK)
        mine = wide[pl.ds(row + FRONT, BLK), :]
        mine = jnp.concatenate([mine, jnp.zeros_like(mine)], axis=1)
        mine = pltpu.roll(mine, FRONT - REACH, 1, stride=1, stride_axis=0)
        high, low = halves(mine)
        fwd[k, 0:BLK, :] = high
        fwd[k, BLK:, :] = low
        near = wide[pl.ds(row, 2 * BLK), :]
        near = jnp.concatenate([near, jnp.zeros_like(near)], axis=1)
        near = pltpu.roll(near, 2 * BLK - (FRONT + REACH), 1, stride=1, stride_axis=0)[:, :BLK]
        near = near / jnp.sum(near, axis=0, keepdims=True)
        high, low = halves(jnp.transpose(near))
        adj[k, 0:BLK, :] = high
        adj[k, BLK:, :] = low

    def product(mat, k, row, field):
        both = jnp.dot(mat[k], field[pl.ds(row, 2 * BLK), :], preferred_element_type=F32)
        return both[:BLK, :BLK] + (both[BLK:, :BLK] + both[:BLK, BLK:])

    def in_groups(step):
        @pl.loop(0, KBLKS // GROUP)
        def _(g):
            blocks = []
            for j in range(GROUP):
                k = g * GROUP + j
                row = pl.multiple_of(k * BLK, BLK)
                blocks.append((row, step(row, k)))
            for row, store in blocks:
                store(row)

    def store_halves(value, field, row):
        high, low = halves(value)
        field[pl.ds(row + FRONT, BLK), 0:BLK] = high
        field[pl.ds(row + FRONT, BLK), BLK:] = low

    def restore(columns, last_block):
        def seen(k):
            return columns[pl.ds(2 * k, 2)].reshape(BLK, BLK)

        def start_block(row, k):
            value = seen(k)

            def store(row):
                est[pl.ds(row, BLK), :] = value
                store_halves(value, est_hl, row)

            return store

        def forward_block(row, k):
            return functools.partial(store_halves, seen(k) / product(fwd, k, row, est_hl), rat_hl)

        def renewed(row, k):
            return est[pl.ds(row, BLK), :] * product(adj, k, row, rat_hl)

        def adjoint_block(row, k):
            value = renewed(row, k)

            def store(row):
                est[pl.ds(row, BLK), :] = value
                store_halves(value, est_hl, row)

            return store

        in_groups(start_block)

        @pl.loop(0, ITERS - 1)
        def _(repeat):
            in_groups(forward_block)
            in_groups(adjoint_block)

        in_groups(forward_block)
        in_groups(lambda row, k: last_block(row, k, renewed(row, k)))

    quarter = TILE // F_DEV
    quarter_group = lanes((quarter, BLK)) // PIECE

    def sum_into(parts):
        def sum_block(row, k, value):
            value = value + pltpu.roll(value, BLK // 2, 1)
            value = value + pltpu.roll(value, BLK // 4, 1)

            def store(row):
                for top in range(2):
                    rows = [value[top * TILE + i * quarter : top * TILE + (i + 1) * quarter] for i in range(F_DEV)]
                    result = rows[0]
                    for i in range(1, F_DEV):
                        result = jnp.where(quarter_group == i, rows[i], result)
                    parts[2 * k + top] = result

            return store

        return sum_block

    def cycle_parts(got):
        for m in range(COLS // BLK // 2):
            blocks = [got[F_DEV * m + j] for j in range(F_DEV)]
            for i in range(F_DEV):
                summed[i * quarter : (i + 1) * quarter, m * BLK : (m + 1) * BLK] = interleave(blocks, i, quarter_group)
        step = COLS // 4
        for m in range(2):
            high, low = halves(summed[:, m * step : (m + 1) * step])
            part = jnp.dot(weights[...], jnp.concatenate([high, low, high], axis=0), preferred_element_type=F32)
            cycles[:, m * step : (m + 1) * step] = part.astype(BF16)

    def add_bins(half, bins, total):
        step = COLS // 4
        for m in range(2):
            place = (2 * half + m) * step
            total = total + turn(cycles[:, m * step : (m + 1) * step], chi[bins[0] : bins[1], place : place + step])
        return total

    for copy in half_0:
        copy.wait()
    restore(columns_0, sum_into(parts_0))
    got_0[tile] = parts_0[tile]
    back_0 = exchange(parts_0, got_0, send_a, recv_a)
    for copy in half_1:
        copy.wait()
    restore(columns_1, sum_into(parts_1))
    got_1[tile] = parts_1[tile]
    back_1 = exchange(parts_1, got_1, send_b, recv_b)
    for copy in back_0:
        copy.wait()
    load.wait()
    cycle_parts(got_0)
    totals = [add_bins(0, bins, jnp.zeros((NB * QB, bins[1] - bins[0]), F32)) for bins in BINS]
    for copy in back_1:
        copy.wait()
    cycle_parts(got_1)

    def reduce_bins(c):
        shared, from_core, mixed, from_x, around, placed, from_z, own, final = chunks[c :: len(BINS)]
        bins = BINS[c]
        total = add_bins(1, bins, totals[c])
        for i in range(NX):
            for j in range(NC):
                top = (i * NC + j) * QB
                shared[j, i] = total[top : top + QB]

        swap = remote(shared.at[1 - core], from_core, send_c.at[c], recv_c.at[c], {"frames": x * NC + 1 - core})
        swap.start()
        yield
        swap.wait()
        mixed[...] = shared[core] + from_core[...]
        copies = []
        for n in range(1, NX):
            to = lax.rem(x + n, NX)
            copy = remote(mixed.at[to], from_x.at[n - 1], send_x.at[c, n - 1], recv_x.at[c, n - 1], {"frames": to * NC + core})
            copy.start()
            copies.append(copy)
        yield
        for copy in copies:
            copy.wait()
        around[y] = mixed[x] + from_x[0] + from_x[1] + from_x[2]
        copies = []
        for n in range(1, NY):
            to = lax.rem(y + n, NY) * NZ + z
            copy = remote(around.at[y], around.at[y], send_y.at[c, n - 1], recv_y.at[c, n - 1], {"rows": to})
            copy.start()
            copies.append(copy)
        yield
        for copy in copies:
            copy.wait()
        every = around[...].reshape(NY * QB, bins[1] - bins[0])
        high, low = halves(every)
        low2 = (every - high.astype(F32) - low.astype(F32)).astype(BF16)
        place = functools.partial(lax.dot_general, dimension_numbers=(((0,), (0,)), ((), ())), preferred_element_type=F32)
        put = place(jnp.concatenate([hits[...]] * 3, axis=0), jnp.concatenate([high, low, low2], axis=0))
        for k in range(NZ):
            placed[k] = put[k * 2 * share : (k + 1) * 2 * share]
        copies = []
        for n in range(1, NZ):
            to = lax.rem(z + n, NZ)
            copy = remote(placed.at[to], from_z.at[n - 1], send_z.at[c, n - 1], recv_z.at[c, n - 1], {"rows": y * NZ + to})
            copy.start()
            copies.append(copy)
        yield
        for copy in copies:
            copy.wait()
        value = placed[z]
        for n in range(NZ - 1):
            value = value + from_z[n]
        own[...] = value
        final[group] = value
        copies = []
        for n in range(1, GROUPS):
            to = lax.rem(group + n, GROUPS)
            copy = remote(own, final.at[group], send_g.at[c, n - 1], recv_g.at[c, n - 1], {"frames": to})
            copy.start()
            copies.append(copy)
        yield
        for copy in copies:
            copy.wait()
        low_half = sublanes((2 * share, bins[1] - bins[0])) < share
        for j in range(GROUPS // 2):
            a, b = final[2 * j], final[2 * j + 1]
            out[8 * j : 8 * j + 8, bins[0] : bins[1]] = jnp.where(low_half, a, pltpu.roll(b, share, 0))
            out[QB + 8 * j : QB + 8 * j + 8, bins[0] : bins[1]] = jnp.where(low_half, pltpu.roll(a, share, 0), b)

    running = [reduce_bins(c) for c in range(len(BINS))]
    while running:
        running = [chunk for chunk in running if next(chunk, True) is None]


def body(observed, kernel, row_shift, cycle_map, cycle_blocks, chi_map):
    vmem = pl.BlockSpec(memory_space=pltpu.VMEM)
    smem = pl.BlockSpec(memory_space=pltpu.SMEM)
    dma = pltpu.SemaphoreType.DMA
    count = len(OTHERS)
    return pl.pallas_call(
        program_kernel,
        name="restore_and_bin",
        out_shape=jax.ShapeDtypeStruct((TILE, CHI), F32),
        in_specs=[vmem, vmem, smem, vmem, smem, pl.BlockSpec(memory_space=pl.ANY)],
        out_specs=vmem,
        scratch_shapes=[pltpu.VMEM((TILES, TILE, BLK), F32)] * 4
        + [
            pltpu.VMEM((TILES, GROUPS, TILE // GROUPS, BLK), F32),
            pltpu.VMEM((TILE // GROUPS, BLK), F32),
            pltpu.VMEM((PADDED, BLK), F32),
            pltpu.VMEM((KBLKS, 2 * BLK, 2 * BLK), BF16),
            pltpu.VMEM((KBLKS, 2 * BLK, 2 * BLK), BF16),
            pltpu.VMEM((ROWS, BLK), F32),
            pltpu.VMEM((PADDED, 2 * BLK), BF16),
            pltpu.VMEM((PADDED, 2 * BLK), BF16),
            pltpu.VMEM((NB * QB, 3 * TILE), BF16),
        ]
        + [pltpu.VMEM((TILES, TILE // F_DEV, BLK), F32)] * 4
        + [
            pltpu.VMEM((CHI, COLS), BF16),
            pltpu.VMEM((TILE, COLS // 2), F32),
            pltpu.VMEM((NB * QB, COLS // 2), BF16),
            pltpu.VMEM((NY, QB, BLK), F32),
            pltpu.VMEM((NY * QB, NZ * 2 * QB // GROUPS), BF16),
        ]
        + [
            pltpu.VMEM((*rows, last - start), F32)
            for rows in (
                (NC, NX, QB), (NX, QB), (NX, QB), (NX - 1, QB), (NY, QB), (NZ, 8), (NZ - 1, 8), (8,), (GROUPS, 8),
            )
            for start, last in BINS
        ]
        + [dma]
        + [dma((n,)) for n in (count, count, count, GROUPS - 1, NY - 1, count, count, len(BINS)) for _ in range(2)]
        + [dma((len(BINS), n)) for n in (NX - 1, NY - 1, NZ - 1, GROUPS - 1) for _ in range(2)],
        compiler_params=pltpu.CompilerParams(collective_id=0, has_side_effects=True, vmem_limit_bytes=VMEM_LIMIT),
    )(observed, kernel, row_shift, cycle_map, cycle_blocks, jnp.swapaxes(chi_map, 1, 2))


def solution(mesh):
    return jax.shard_map(
        body,
        mesh=mesh,
        in_specs=(
            P("frames", "rows", None),
            P("rows", None),
            P("rows"),
            P("rows", None),
            P("rows", None),
            P("rows", None, None),
        ),
        out_specs=P("rows", None),
        check_vma=False,
    )
```
